1024 devices in a mesh: lon: 32 (over z_hi, y), lat: 16 (over z_lo, x), rad: 2 (over core).
Axes of the slice: x: 8, y: 8, z: 8 (z_hi: 4, z_lo: 2; z = z_hi * 2 + z_lo), core: 2. Of those that a mesh axis runs over, the one named last changes fastest.
Arguments:
- adj_now: float32 [16, 512, 4096], P('rad', 'lat', 'lon'), may hold values from -6 to 6
- adj_next: float32 [16, 512, 4096], P('rad', 'lat', 'lon'), may hold values from -6 to 6
- fwd_now: float32 [16, 512, 4096], P('rad', 'lat', 'lon'), may hold values from -6 to 6
- fwd_next: float32 [16, 512, 4096], P('rad', 'lat', 'lon'), may hold values from -6 to 6
- stiffness: float32 [16, 512, 4096], P('rad', 'lat', 'lon'), may hold values from 0.04 to 0.15
- buoyancy: float32 [16, 512, 4096], P('rad', 'lat', 'lon'), may hold values from 0.6 to 1.5
- kernel_bulk_in: float32 [16, 512, 4096], P('rad', 'lat', 'lon'), may hold values from -6 to 6
- kernel_density_in: float32 [16, 512, 4096], P('rad', 'lat', 'lon'), may hold values from -6 to 6
Outputs:
- adj_out_now: float32 [16, 512, 4096], P('rad', 'lat', 'lon')
- adj_out_next: float32 [16, 512, 4096], P('rad', 'lat', 'lon')
- fwd_out_now: float32 [16, 512, 4096], P('rad', 'lat', 'lon')
- fwd_out_next: float32 [16, 512, 4096], P('rad', 'lat', 'lon')
- kernel_bulk: float32 [16, 512, 4096], P('rad', 'lat', 'lon')
- kernel_density: float32 [16, 512, 4096], P('rad', 'lat', 'lon')
The draws below stay inside these ranges and needn't reach their ends.
All inputs are finite; a program needn't handle non-finite values.
Results may differ from the reference program's by a relative error of at most 0.00002.
Values sent between devices are 32-bit elements; how exact they have to be, the bound alone decides.
A program may use at most 32 MiB of HBM per device.

```python
import math
import jax
import jax.numpy as jnp
from jax import lax

STEPS = 2
NRAD = 16
NLAT = 512
NLON = 4096


def block_scale(stream_key, extent, cuts, smallest, high):
    loudness = 1.0
    for axis_at, shards_of in cuts:
        steps = jax.random.uniform(jax.random.fold_in(jax.random.fold_in(stream_key, 6), axis_at), (shards_of,), jnp.float32, smallest / len(cuts), high / len(cuts))
        loudness = loudness * jnp.repeat(jnp.exp(steps), extent[axis_at] // shards_of).reshape((-1,) + (1,) * (len(extent) - 1 - axis_at))
    return loudness


def normal_values(rng, extent, spread, bound, shards=(), kind=jnp.bfloat16):
    loudness = block_scale(rng, extent, shards, -0.22, 0.18) if shards else 1.0
    drawn = jax.random.normal(rng, extent, jnp.float32) * spread * loudness
    return jnp.minimum(jnp.maximum(drawn, -bound), bound).astype(kind)


def setup_inputs(seed: int = 0) -> dict:
    key_of = jax.random.split(jax.random.key(seed), 9)
    return {
        "adj_now": normal_values(key_of[0], (NRAD, NLAT, NLON), 1.0, 6.0, ((0, 2), (1, 16), (2, 32)), jnp.float32),
        "adj_next": normal_values(key_of[1], (NRAD, NLAT, NLON), 1.0, 6.0, ((0, 2), (1, 16), (2, 32)), jnp.float32),
        "fwd_now": normal_values(key_of[2], (NRAD, NLAT, NLON), 1.0, 6.0, ((0, 2), (1, 16), (2, 32)), jnp.float32),
        "fwd_next": normal_values(key_of[3], (NRAD, NLAT, NLON), 1.0, 6.0, ((0, 2), (1, 16), (2, 32)), jnp.float32),
        "stiffness": jnp.clip(0.04 + 0.11000001 * jax.random.uniform(key_of[4], (NRAD, NLAT, NLON), jnp.float32) ** block_scale(key_of[4], (NRAD, NLAT, NLON), ((0, 2), (1, 16), (2, 32)), -0.2, 0.2), 0.04, 0.15),
        "buoyancy": jnp.clip(jnp.exp(math.log(1.5) - 0.9162907 * jax.random.uniform(key_of[5], (NRAD, NLAT, NLON), jnp.float32) ** block_scale(key_of[5], (NRAD, NLAT, NLON), ((0, 2), (1, 16), (2, 32)), -0.2, 0.2)), 0.6, 1.5),
        "kernel_bulk_in": normal_values(key_of[6], (NRAD, NLAT, NLON), 1.0, 6.0, ((0, 2), (1, 16), (2, 32)), jnp.float32),
        "kernel_density_in": normal_values(key_of[7], (NRAD, NLAT, NLON), 1.0, 6.0, ((0, 2), (1, 16), (2, 32)), jnp.float32),
    }


coef_near = 9.0 / 8.0
coef_far = -1.0 / 24.0


def pad_all(field, width):
    field = jnp.pad(field, ((0, 0), (0, 0), (width, width)), mode="wrap")
    return jnp.pad(field, ((width, width), (width, width), (0, 0)))


def piece(field, first, last, axis_num):
    return lax.slice_in_dim(field, first, last, axis=axis_num)


def operate(adj_pad, fwd_pad, buoy_pad):
    lap_adj = None
    lap_fwd = None
    rho_term = None
    for dim_index in range(3):
        arrays = []
        for source in (adj_pad, fwd_pad, buoy_pad):
            for other in range(3):
                if other != dim_index:
                    source = piece(source, 3, source.shape[other] - 3, other)
            arrays.append(source)
        adj_part, fwd_part, buoy_part = arrays
        length = adj_part.shape[dim_index]

        def faces(field):
            near = piece(field, 2, length - 1, dim_index) - piece(field, 1, length - 2, dim_index)
            far = piece(field, 3, length, dim_index) - piece(field, 0, length - 3, dim_index)
            return coef_near * near + coef_far * far

        face_buoy = 0.5 * (piece(buoy_part, 1, length - 2, dim_index) + piece(buoy_part, 2, length - 1, dim_index))
        grad_adj = faces(adj_part)
        grad_fwd = faces(fwd_part)
        count = length - 3

        def diverge(flux):
            near = piece(flux, 2, count - 1, dim_index) - piece(flux, 1, count - 2, dim_index)
            far = piece(flux, 3, count, dim_index) - piece(flux, 0, count - 3, dim_index)
            return coef_near * near + coef_far * far

        term_adj = diverge(face_buoy * grad_adj)
        term_fwd = diverge(face_buoy * grad_fwd)
        product = face_buoy * grad_adj * grad_fwd
        term_rho = 0.5 * (piece(product, 2, count - 1, dim_index) + piece(product, 1, count - 2, dim_index))
        if lap_adj is None:
            lap_adj, lap_fwd, rho_term = term_adj, term_fwd, term_rho
        else:
            lap_adj = lap_adj + term_adj
            lap_fwd = lap_fwd + term_fwd
            rho_term = rho_term + term_rho
    return lap_adj, lap_fwd, rho_term


def reference(adj_now, adj_next, fwd_now, fwd_next, stiffness, buoyancy, kernel_bulk_in, kernel_density_in):
    buoy_pad = pad_all(buoyancy, 3)
    kernel_bulk = kernel_bulk_in
    kernel_density = kernel_density_in
    for turn_index in range(STEPS):
        lap_adj, lap_fwd, rho_term = operate(pad_all(adj_now, 3), pad_all(fwd_now, 3), buoy_pad)
        kernel_bulk = kernel_bulk + adj_now * (stiffness * lap_fwd)
        kernel_density = kernel_density + rho_term
        new_adj = 2.0 * adj_now - adj_next + stiffness * lap_adj
        new_fwd = 2.0 * fwd_now - fwd_next + stiffness * lap_fwd
        adj_next, adj_now = adj_now, new_adj
        fwd_next, fwd_now = fwd_now, new_fwd
    return adj_now, adj_next, fwd_now, fwd_next, kernel_bulk, kernel_density
```

```python
import jax
import jax.numpy as jnp
from jax import lax
from jax.experimental import pallas as pl
from jax.experimental.pallas import tpu as pltpu
from jax.sharding import PartitionSpec as P

MESH = pl.DeviceIdType.MESH

near = 9.0 / 8.0
far = -1.0 / 24.0
half_near = near / 2
half_far = far / 2

LOW = 8
WIDE = 3


def kernel(
    nrad, nlat, nlon, counts,
    adj_now, adj_next, fwd_now, fwd_next, stiffness, buoyancy, bulk_in, density_in,
    out_adj_now, out_adj_next, out_fwd_now, out_fwd_next, out_bulk, out_density,
    first, second, side, total, flux, final,
    lon_send, lon_recv, lat_send, lat_recv,
    load_sem, save_sem, lon_ssem, lon_rsem, lat_ssem, lat_rsem, rad_ssem, rad_rsem,
):
    lons, lats, _ = counts
    lon = lax.axis_index("lon")
    lat = lax.axis_index("lat")
    core = lax.axis_index("rad")
    east = lax.rem(lon + 1, lons)
    west = lax.rem(lon + lons - 1, lons)
    other = 1 - core
    has_south = lat > 0
    has_north = lat < lats - 1

    barrier = pltpu.get_barrier_semaphore()

    def greet(where):
        pl.semaphore_signal(barrier, inc=1, device_id=where, device_id_type=MESH)

    greet({"lon": east})
    greet({"lon": west})
    greet({"rad": other})

    @pl.when(has_south)
    def _():
        greet({"lat": lat - 1})

    @pl.when(has_north)
    def _():
        greet({"lat": lat + 1})

    inside = (pl.ds(WIDE, nrad), pl.ds(LOW, nlat))
    sources = (adj_now, fwd_now, buoyancy, stiffness, adj_next, fwd_next, bulk_in, density_in)
    loads = []
    for k, source in enumerate(sources):
        target = first.at[(k,) + inside] if k < 3 else side.at[k - 3]
        loads.append(pltpu.make_async_copy(source, target, load_sem.at[k]))
        loads[-1].start()

    edge = 11 * core
    for block, fields in ((first, 3), (second, 2)):
        for f in range(fields):
            block[f, pl.ds(edge, WIDE)] = jnp.zeros((WIDE, nlat + 16, nlon), jnp.float32)

    @pl.when(jnp.logical_not(has_south))
    def _():
        for step in range(2):
            lat_recv[step, 0] = jnp.zeros(lat_recv.shape[2:], jnp.float32)

    @pl.when(jnp.logical_not(has_north))
    def _():
        for step in range(2):
            lat_recv[step, 1] = jnp.zeros(lat_recv.shape[2:], jnp.float32)

    lane = lax.broadcasted_iota(jnp.int32, (nlat, nlon), 1)
    group = lax.shift_right_logical(lane * 43, 7)

    def pack(block, fields, step):
        to_east = jnp.zeros((nlat, nlon), jnp.float32)
        to_west = jnp.zeros((nlat, nlon), jnp.float32)
        for f in range(fields):
            for r in range(nrad):
                n = f * nrad + r
                turned = pltpu.roll(block[f, WIDE + r, pl.ds(LOW, nlat)], (3 * n - 125) % 128, 1)
                to_east = jnp.where(group == n, turned, to_east)
                to_west = jnp.where(group == n + 1, turned, to_west)
                lat_send[step, 0, pl.ds(3 * n, 3)] = block[f, WIDE + r, pl.ds(LOW + nlat - 3, 3)]
                lat_send[step, 1, pl.ds(3 * n, 3)] = block[f, WIDE + r, pl.ds(LOW, 3)]
        lon_send[step, 0] = to_east
        lon_send[step, 1] = to_west

    def lon_copy(step, way, where):
        return pltpu.make_async_remote_copy(
            lon_send.at[step, way], lon_recv.at[step, way],
            lon_ssem.at[step, way], lon_rsem.at[step, way],
            device_id={"lon": where}, device_id_type=MESH,
        )

    def lat_copy(step, way, where, fields):
        rows = pl.ds(0, fields * nrad * 3)
        return pltpu.make_async_remote_copy(
            lat_send.at[step, way, rows], lat_recv.at[step, way, rows],
            lat_ssem.at[step, way], lat_rsem.at[step, way],
            device_id={"lat": where}, device_id_type=MESH,
        )

    def rad_copy(step, block):
        return pltpu.make_async_remote_copy(
            block.at[:, pl.ds(8 - 5 * core, WIDE), pl.ds(LOW, nlat)],
            block.at[:, pl.ds(11 * core, WIDE), pl.ds(LOW, nlat)],
            rad_ssem.at[step], rad_rsem.at[step],
            device_id={"rad": other}, device_id_type=MESH,
        )

    def send(step, block, fields):
        lon_copy(step, 0, east).start()
        lon_copy(step, 1, west).start()

        @pl.when(has_north)
        def _():
            lat_copy(step, 0, lat + 1, fields).start()

        @pl.when(has_south)
        def _():
            lat_copy(step, 1, lat - 1, fields).start()

        rad_copy(step, block).start()

    def wait_rad(step, block):
        rad_copy(step, block).wait_recv()

    def wait_lat(step, fields):
        @pl.when(has_south)
        def _():
            lat_copy(step, 0, lat - 1, fields).wait_recv()

        @pl.when(has_north)
        def _():
            lat_copy(step, 1, lat + 1, fields).wait_recv()

    def wait_lon(step):
        lon_copy(step, 0, west).wait_recv()
        lon_copy(step, 1, east).wait_recv()

    def wait_sent(step, block, fields):
        lon_copy(step, 0, east).wait_send()
        lon_copy(step, 1, west).wait_send()

        @pl.when(has_north)
        def _():
            lat_copy(step, 0, lat + 1, fields).wait_send()

        @pl.when(has_south)
        def _():
            lat_copy(step, 1, lat - 1, fields).wait_send()

        rad_copy(step, block).wait_send()

    def along_rad(block):
        for t in range(nlat // 8):
            rows = pl.ds(LOW + 8 * t, 8)
            adj, fwd, buoy = block[0, :, rows], block[1, :, rows], first[2, :, rows]

            def faces(p):
                return near * (p[2:13] - p[1:12]) + far * (p[3:14] - p[0:11])

            both = buoy[1:12] + buoy[2:13]
            grad_fwd = faces(fwd)
            flux_adj, flux_fwd = both * faces(adj), both * grad_fwd
            product = flux_adj * grad_fwd

            def diverge(q):
                return half_near * (q[2:10] - q[1:9]) + half_far * (q[3:11] - q[0:8])

            here = pl.ds(8 * t, 8)
            total[0, :, here] = diverge(flux_adj)
            total[1, :, here] = diverge(flux_fwd)
            total[2, :, here] = product[1:9] + product[2:10]

    def along_lat(step, block, fields):
        for f in range(fields):
            for r in range(nrad):
                n = f * nrad + r
                block[f, WIDE + r, pl.ds(LOW - 3, 3)] = lat_recv[step, 0, pl.ds(3 * n, 3)]
                block[f, WIDE + r, pl.ds(LOW + nlat, 3)] = lat_recv[step, 1, pl.ds(3 * n, 3)]
        rows = nlat + 8
        for r in range(nrad):
            def at(ref, f, k):
                return ref[f, WIDE + r, pl.ds(LOW - 2 + k, rows)]

            def faces(f):
                return near * (at(block, f, 1) - at(block, f, 0)) + far * (
                    at(block, f, 2) - at(block, f, -1)
                )

            both = at(first, 2, 0) + at(first, 2, 1)
            grad_fwd = faces(1)
            flux_adj = both * faces(0)
            flux[r, 0] = flux_adj
            flux[r, 1] = both * grad_fwd
            flux[r, 2] = flux_adj * grad_fwd

            def moved(f, k):
                return flux[r, f, pl.ds(2 + k, nlat)]

            for f in range(2):
                total[f, r] += half_near * (moved(f, 0) - moved(f, -1)) + half_far * (
                    moved(f, 1) - moved(f, -2)
                )
            total[2, r] += moved(2, 0) + moved(2, -1)

    def ahead(x, h, k):
        return pltpu.roll(jnp.where(lane < k, h, x), 128 - k, 1)

    def behind(x, h, k):
        return pltpu.roll(jnp.where(lane >= 128 - k, h, x), k, 1)

    def along_lon(step, block, r):
        def halo(at_step, f):
            turn = (125 - 3 * (f * nrad + r)) % 128
            return jnp.where(
                lane < 64,
                pltpu.roll(lon_recv[at_step, 1], turn, 1),
                pltpu.roll(lon_recv[at_step, 0], turn, 1),
            )

        def faces(x, h):
            return near * (ahead(x, h, 1) - x) + far * (ahead(x, h, 2) - behind(x, h, 1))

        def diverge(x, h):
            return half_near * (x - behind(x, h, 1)) + half_far * (
                ahead(x, h, 1) - behind(x, h, 2)
            )

        here = (WIDE + r, pl.ds(LOW, nlat))
        adj, fwd, buoy = block[(0,) + here], block[(1,) + here], first[(2,) + here]
        adj_h, fwd_h, buoy_h = halo(step, 0), halo(step, 1), halo(0, 2)
        both, both_h = buoy + ahead(buoy, buoy_h, 1), buoy_h + ahead(buoy_h, buoy, 1)
        grad, grad_h = faces(fwd, fwd_h), faces(fwd_h, fwd)
        q_adj, q_adj_h = both * faces(adj, adj_h), both_h * faces(adj_h, adj)
        q_fwd, q_fwd_h = both * grad, both_h * grad_h
        product, product_h = q_adj * grad, q_adj_h * grad_h
        lap_adj = stiff_ref[r] * (total[0, r] + diverge(q_adj, q_adj_h))
        lap_fwd = stiff_ref[r] * (total[1, r] + diverge(q_fwd, q_fwd_h))
        rho = total[2, r] + (product + behind(product, product_h, 1))
        return adj, fwd, lap_adj, lap_fwd, rho

    stiff_ref, adj_next_ref, fwd_next_ref, bulk_ref, density_ref = (side.at[k] for k in range(5))

    for k in range(3):
        loads[k].wait()
    pack(first, 3, 0)
    pl.semaphore_wait(barrier, 3 + has_south.astype(jnp.int32) + has_north.astype(jnp.int32))
    send(0, first, 3)
    for k in range(3, 8):
        loads[k].wait()

    wait_rad(0, first)
    along_rad(first)
    wait_lat(0, 3)
    along_lat(0, first, 3)
    wait_lon(0)
    for r in range(nrad):
        adj, fwd, lap_adj, lap_fwd, rho = along_lon(0, first, r)
        bulk_ref[r] += adj * lap_fwd
        density_ref[r] += 0.25 * rho
        second[0, WIDE + r, pl.ds(LOW, nlat)] = 2.0 * adj - adj_next_ref[r] + lap_adj
        second[1, WIDE + r, pl.ds(LOW, nlat)] = 2.0 * fwd - fwd_next_ref[r] + lap_fwd

    pack(second, 2, 1)
    send(1, second, 2)
    saves = [
        pltpu.make_async_copy(second.at[(0,) + inside], out_adj_next, save_sem.at[0]),
        pltpu.make_async_copy(second.at[(1,) + inside], out_fwd_next, save_sem.at[1]),
        pltpu.make_async_copy(final.at[0], out_adj_now, save_sem.at[2]),
        pltpu.make_async_copy(final.at[1], out_fwd_now, save_sem.at[3]),
        pltpu.make_async_copy(bulk_ref, out_bulk, save_sem.at[4]),
        pltpu.make_async_copy(density_ref, out_density, save_sem.at[5]),
    ]
    saves[0].start()
    saves[1].start()

    wait_rad(1, second)
    along_rad(second)
    wait_lat(1, 2)
    along_lat(1, second, 2)
    wait_lon(1)
    for r in range(nrad):
        adj, fwd, lap_adj, lap_fwd, rho = along_lon(1, second, r)
        bulk_ref[r] += adj * lap_fwd
        density_ref[r] += 0.25 * rho
        final[0, r] = 2.0 * adj - first[0, WIDE + r, pl.ds(LOW, nlat)] + lap_adj
        final[1, r] = 2.0 * fwd - first[1, WIDE + r, pl.ds(LOW, nlat)] + lap_fwd
    for save in saves[2:]:
        save.start()
    wait_sent(0, first, 3)
    wait_sent(1, second, 2)
    for save in saves:
        save.wait()


def solution(mesh):
    counts = (mesh.shape["lon"], mesh.shape["lat"], mesh.shape["rad"])

    def shards(*blocks):
        nrad, nlat, nlon = blocks[0].shape
        rows, f32, dma = nlat + 16, jnp.float32, pltpu.SemaphoreType.DMA
        return pl.pallas_call(
            lambda *refs: kernel(nrad, nlat, nlon, counts, *refs),
            out_shape=(jax.ShapeDtypeStruct(blocks[0].shape, f32),) * 6,
            in_specs=[pl.BlockSpec(memory_space=pl.ANY)] * 8,
            out_specs=(pl.BlockSpec(memory_space=pl.ANY),) * 6,
            scratch_shapes=[
                pltpu.VMEM((3, nrad + 2 * WIDE, rows, nlon), f32),
                pltpu.VMEM((2, nrad + 2 * WIDE, rows, nlon), f32),
                pltpu.VMEM((5, nrad, nlat, nlon), f32),
                pltpu.VMEM((3, nrad, nlat, nlon), f32),
                pltpu.VMEM((nrad, 3, nlat + 8, nlon), f32),
                pltpu.VMEM((2, nrad, nlat, nlon), f32),
                pltpu.VMEM((2, 2, nlat, nlon), f32),
                pltpu.VMEM((2, 2, nlat, nlon), f32),
                pltpu.VMEM((2, 2, 9 * nrad, nlon), f32),
                pltpu.VMEM((2, 2, 9 * nrad, nlon), f32),
                dma((8,)), dma((6,)),
                dma((2, 2)), dma((2, 2)), dma((2, 2)), dma((2, 2)), dma((2,)), dma((2,)),
            ],
            compiler_params=pltpu.CompilerParams(collective_id=0, has_side_effects=True),
            name="steps",
        )(*blocks)

    spec = P("rad", "lat", "lon")
    return jax.shard_map(
        shards, mesh=mesh, in_specs=(spec,) * 8, out_specs=(spec,) * 6, check_vma=False
    )
```

```python
import jax
import jax.numpy as jnp
from jax import lax
from jax.experimental import pallas as pl
from jax.experimental.pallas import tpu as pltpu
from jax.sharding import PartitionSpec as P

MESH = pl.DeviceIdType.MESH

near = 9.0 / 8.0
far = -1.0 / 24.0
half_near = near / 2
half_far = far / 2

LOW = 8
WIDE = 3


def kernel(
    nrad, nlat, nlon, counts,
    adj_now, adj_next, fwd_now, fwd_next, stiffness, buoyancy, bulk_in, density_in,
    out_adj_now, out_adj_next, out_fwd_now, out_fwd_next, out_bulk, out_density,
    first, second, side, total, flux,
    lon_send, lon_recv, lat_send, lat_recv,
    load_sem, lon_ssem, lon_rsem, lat_ssem, lat_rsem, rad_ssem, rad_rsem,
):
    lons, lats, _ = counts
    lon = lax.axis_index("lon")
    lat = lax.axis_index("lat")
    core = lax.axis_index("rad")
    east = lax.rem(lon + 1, lons)
    west = lax.rem(lon + lons - 1, lons)
    other = 1 - core
    has_south = lat > 0
    has_north = lat < lats - 1

    barrier = pltpu.get_barrier_semaphore()

    def greet(where):
        pl.semaphore_signal(barrier, inc=1, device_id=where, device_id_type=MESH)

    greet({"lon": east})
    greet({"lon": west})
    greet({"rad": other})

    @pl.when(has_south)
    def _():
        greet({"lat": lat - 1})

    @pl.when(has_north)
    def _():
        greet({"lat": lat + 1})

    inside = (pl.ds(WIDE, nrad), pl.ds(LOW, nlat))
    sources = (adj_now, fwd_now, buoyancy, stiffness, adj_next, fwd_next, bulk_in, density_in)
    loads = []
    for k, source in enumerate(sources):
        target = first.at[(k,) + inside] if k < 3 else side.at[k - 3]
        loads.append(pltpu.make_async_copy(source, target, load_sem.at[k]))
        loads[-1].start()

    edge = 11 * core
    for block, fields in ((first, 3), (second, 2)):
        for f in range(fields):
            block[f, pl.ds(edge, WIDE)] = jnp.zeros((WIDE, nlat + 16, nlon), jnp.float32)

    @pl.when(jnp.logical_not(has_south))
    def _():
        for step in range(2):
            lat_recv[step, 0] = jnp.zeros(lat_recv.shape[2:], jnp.float32)

    @pl.when(jnp.logical_not(has_north))
    def _():
        for step in range(2):
            lat_recv[step, 1] = jnp.zeros(lat_recv.shape[2:], jnp.float32)

    lane = lax.broadcasted_iota(jnp.int32, (nlat, nlon), 1)
    group = lax.shift_right_logical(lane * 43, 7)

    def pack(block, fields, step):
        to_east = jnp.zeros((nlat, nlon), jnp.float32)
        to_west = jnp.zeros((nlat, nlon), jnp.float32)
        for f in range(fields):
            for r in range(nrad):
                n = f * nrad + r
                turned = pltpu.roll(block[f, WIDE + r, pl.ds(LOW, nlat)], (3 * n - 125) % 128, 1)
                to_east = jnp.where(group == n, turned, to_east)
                to_west = jnp.where(group == n + 1, turned, to_west)
                lat_send[step, 0, pl.ds(3 * n, 3)] = block[f, WIDE + r, pl.ds(LOW + nlat - 3, 3)]
                lat_send[step, 1, pl.ds(3 * n, 3)] = block[f, WIDE + r, pl.ds(LOW, 3)]
        lon_send[step, 0] = to_east
        lon_send[step, 1] = to_west

    def lon_copy(step, way, where):
        return pltpu.make_async_remote_copy(
            lon_send.at[step, way], lon_recv.at[step, way],
            lon_ssem.at[step, way], lon_rsem.at[step, way],
            device_id={"lon": where}, device_id_type=MESH,
        )

    def lat_copy(step, way, where, fields):
        rows = pl.ds(0, fields * nrad * 3)
        return pltpu.make_async_remote_copy(
            lat_send.at[step, way, rows], lat_recv.at[step, way, rows],
            lat_ssem.at[step, way], lat_rsem.at[step, way],
            device_id={"lat": where}, device_id_type=MESH,
        )

    def rad_copy(step, block):
        return pltpu.make_async_remote_copy(
            block.at[:, pl.ds(8 - 5 * core, WIDE), pl.ds(LOW, nlat)],
            block.at[:, pl.ds(11 * core, WIDE), pl.ds(LOW, nlat)],
            rad_ssem.at[step], rad_rsem.at[step],
            device_id={"rad": other}, device_id_type=MESH,
        )

    def send(step, block, fields):
        lon_copy(step, 0, east).start()
        lon_copy(step, 1, west).start()

        @pl.when(has_north)
        def _():
            lat_copy(step, 0, lat + 1, fields).start()

        @pl.when(has_south)
        def _():
            lat_copy(step, 1, lat - 1, fields).start()

        rad_copy(step, block).start()

    def wait_rad(step, block):
        rad_copy(step, block).wait_recv()

    def wait_lat(step, fields):
        @pl.when(has_south)
        def _():
            lat_copy(step, 0, lat - 1, fields).wait_recv()

        @pl.when(has_north)
        def _():
            lat_copy(step, 1, lat + 1, fields).wait_recv()

    def wait_lon(step):
        lon_copy(step, 0, west).wait_recv()
        lon_copy(step, 1, east).wait_recv()

    def wait_sent(step, block, fields):
        lon_copy(step, 0, east).wait_send()
        lon_copy(step, 1, west).wait_send()

        @pl.when(has_north)
        def _():
            lat_copy(step, 0, lat + 1, fields).wait_send()

        @pl.when(has_south)
        def _():
            lat_copy(step, 1, lat - 1, fields).wait_send()

        rad_copy(step, block).wait_send()

    def along_rad(block):
        for t in range(nlat // 8):
            rows = pl.ds(LOW + 8 * t, 8)
            adj, fwd, buoy = block[0, :, rows], block[1, :, rows], first[2, :, rows]

            def faces(p):
                return near * (p[2:13] - p[1:12]) + far * (p[3:14] - p[0:11])

            both = buoy[1:12] + buoy[2:13]
            grad_fwd = faces(fwd)
            flux_adj, flux_fwd = both * faces(adj), both * grad_fwd
            product = flux_adj * grad_fwd

            def diverge(q):
                return half_near * (q[2:10] - q[1:9]) + half_far * (q[3:11] - q[0:8])

            here = pl.ds(8 * t, 8)
            total[0, :, here] = diverge(flux_adj)
            total[1, :, here] = diverge(flux_fwd)
            total[2, :, here] = product[1:9] + product[2:10]

    def along_lat(step, block, fields):
        for f in range(fields):
            for r in range(nrad):
                n = f * nrad + r
                block[f, WIDE + r, pl.ds(LOW - 3, 3)] = lat_recv[step, 0, pl.ds(3 * n, 3)]
                block[f, WIDE + r, pl.ds(LOW + nlat, 3)] = lat_recv[step, 1, pl.ds(3 * n, 3)]
        rows = nlat + 8
        for r in range(nrad):
            def at(ref, f, k):
                return ref[f, WIDE + r, pl.ds(LOW - 2 + k, rows)]

            def faces(f):
                return near * (at(block, f, 1) - at(block, f, 0)) + far * (
                    at(block, f, 2) - at(block, f, -1)
                )

            both = at(first, 2, 0) + at(first, 2, 1)
            grad_fwd = faces(1)
            flux_adj = both * faces(0)
            flux[r, 0] = flux_adj
            flux[r, 1] = both * grad_fwd
            flux[r, 2] = flux_adj * grad_fwd

            def moved(f, k):
                return flux[r, f, pl.ds(2 + k, nlat)]

            for f in range(2):
                total[f, r] += half_near * (moved(f, 0) - moved(f, -1)) + half_far * (
                    moved(f, 1) - moved(f, -2)
                )
            total[2, r] += moved(2, 0) + moved(2, -1)

    def ahead(x, h, k):
        return pltpu.roll(jnp.where(lane < k, h, x), 128 - k, 1)

    def behind(x, h, k):
        return pltpu.roll(jnp.where(lane >= 128 - k, h, x), k, 1)

    def along_lon(step, block, r):
        def halo(at_step, f):
            turn = (125 - 3 * (f * nrad + r)) % 128
            return jnp.where(
                lane < 64,
                pltpu.roll(lon_recv[at_step, 1], turn, 1),
                pltpu.roll(lon_recv[at_step, 0], turn, 1),
            )

        def faces(x, h):
            step, step_h = x - behind(x, h, 1), h - behind(h, x, 1)

            def smooth(d, e):
                return (near + far) * d + far * (ahead(d, e, 1) + behind(d, e, 1))

            return smooth(step, step_h), smooth(step_h, step)

        def diverge(q, h):
            t, t_h = behind(q, h, 1), behind(h, q, 1)
            v, v_h = half_near * t + half_far * q, half_near * t_h + half_far * h
            return ahead(v, v_h, 2) - (half_far * t + half_near * q)

        here = (WIDE + r, pl.ds(LOW, nlat))
        adj, fwd, buoy = block[(0,) + here], block[(1,) + here], first[(2,) + here]
        buoy_h = halo(0, 2)
        both, both_h = buoy + behind(buoy, buoy_h, 1), buoy_h + behind(buoy_h, buoy, 1)
        grad, grad_h = faces(fwd, halo(step, 1))
        slope, slope_h = faces(adj, halo(step, 0))
        q_adj, q_adj_h = both * slope, both_h * slope_h
        q_fwd, q_fwd_h = both * grad, both_h * grad_h
        product, product_h = q_adj * grad, q_adj_h * grad_h
        lap_adj = stiff_ref[r] * (total[0, r] + diverge(q_adj, q_adj_h))
        lap_fwd = stiff_ref[r] * (total[1, r] + diverge(q_fwd, q_fwd_h))
        rho = total[2, r] + (product + ahead(product, product_h, 1))
        return adj, fwd, lap_adj, lap_fwd, rho

    stiff_ref, adj_next_ref, fwd_next_ref, bulk_ref, density_ref = (side.at[k] for k in range(5))

    for k in range(3):
        loads[k].wait()
    pack(first, 3, 0)
    pl.semaphore_wait(barrier, 3 + has_south.astype(jnp.int32) + has_north.astype(jnp.int32))
    send(0, first, 3)
    for k in range(3, 8):
        loads[k].wait()

    wait_rad(0, first)
    along_rad(first)
    wait_lat(0, 3)
    along_lat(0, first, 3)
    wait_lon(0)
    for r in range(nrad):
        adj, fwd, lap_adj, lap_fwd, rho = along_lon(0, first, r)
        bulk_ref[r] += adj * lap_fwd
        density_ref[r] += 0.25 * rho
        second[0, WIDE + r, pl.ds(LOW, nlat)] = 2.0 * adj - adj_next_ref[r] + lap_adj
        second[1, WIDE + r, pl.ds(LOW, nlat)] = 2.0 * fwd - fwd_next_ref[r] + lap_fwd

    pack(second, 2, 1)
    send(1, second, 2)
    out_adj_next[...] = second[(0,) + inside]
    out_fwd_next[...] = second[(1,) + inside]

    wait_rad(1, second)
    along_rad(second)
    wait_lat(1, 2)
    along_lat(1, second, 2)
    wait_lon(1)
    for r in range(nrad):
        adj, fwd, lap_adj, lap_fwd, rho = along_lon(1, second, r)
        out_bulk[r] = bulk_ref[r] + adj * lap_fwd
        out_density[r] = density_ref[r] + 0.25 * rho
        out_adj_now[r] = 2.0 * adj - first[0, WIDE + r, pl.ds(LOW, nlat)] + lap_adj
        out_fwd_now[r] = 2.0 * fwd - first[1, WIDE + r, pl.ds(LOW, nlat)] + lap_fwd
    wait_sent(0, first, 3)
    wait_sent(1, second, 2)


def write_out(*refs):
    results, outs, sems = refs[:6], refs[6:12], refs[12]
    copies = [
        pltpu.make_async_copy(result, out, sems.at[k])
        for k, (result, out) in enumerate(zip(results, outs))
    ]
    for copy in copies:
        copy.start()
    for copy in copies:
        copy.wait()


def solution(mesh):
    counts = (mesh.shape["lon"], mesh.shape["lat"], mesh.shape["rad"])

    def shards(*blocks):
        nrad, nlat, nlon = blocks[0].shape
        rows, f32, dma = nlat + 16, jnp.float32, pltpu.SemaphoreType.DMA
        held = pl.pallas_call(
            lambda *refs: kernel(nrad, nlat, nlon, counts, *refs),
            out_shape=(pltpu.VMEM(blocks[0].shape, f32),) * 6,
            in_specs=[pl.BlockSpec(memory_space=pl.ANY)] * 8,
            out_specs=(pl.BlockSpec(memory_space=pltpu.VMEM),) * 6,
            scratch_shapes=[
                pltpu.VMEM((3, nrad + 2 * WIDE, rows, nlon), f32),
                pltpu.VMEM((2, nrad + 2 * WIDE, rows, nlon), f32),
                pltpu.VMEM((5, nrad, nlat, nlon), f32),
                pltpu.VMEM((3, nrad, nlat, nlon), f32),
                pltpu.VMEM((nrad, 3, nlat + 8, nlon), f32),
                pltpu.VMEM((2, 2, nlat, nlon), f32),
                pltpu.VMEM((2, 2, nlat, nlon), f32),
                pltpu.VMEM((2, 2, 9 * nrad, nlon), f32),
                pltpu.VMEM((2, 2, 9 * nrad, nlon), f32),
                dma((8,)),
                dma((2, 2)), dma((2, 2)), dma((2, 2)), dma((2, 2)), dma((2,)), dma((2,)),
            ],
            compiler_params=pltpu.CompilerParams(collective_id=0, has_side_effects=True),
            name="steps",
        )(*blocks)
        return pl.pallas_call(
            write_out,
            out_shape=(jax.ShapeDtypeStruct(blocks[0].shape, f32),) * 6,
            in_specs=[pl.BlockSpec(memory_space=pltpu.VMEM)] * 6,
            out_specs=(pl.BlockSpec(memory_space=pl.ANY),) * 6,
            scratch_shapes=[dma((6,))],
            name="write_out",
        )(*(pltpu.with_memory_space_constraint(x, pltpu.VMEM) for x in held))

    spec = P("rad", "lat", "lon")
    return jax.shard_map(
        shards, mesh=mesh, in_specs=(spec,) * 8, out_specs=(spec,) * 6, check_vma=False
    )
```

```python
import jax
import jax.numpy as jnp
from jax import lax
from jax.experimental import pallas as pl
from jax.experimental.pallas import tpu as pltpu
from jax.sharding import PartitionSpec as P

MESH = pl.DeviceIdType.MESH

near = 9.0 / 8.0
far = -1.0 / 24.0
half_near = near / 2
half_far = far / 2

LOW = 8
WIDE = 3


def kernel(
    nrad, nlat, nlon, counts,
    adj_now, adj_next, fwd_now, fwd_next, stiffness, buoyancy, bulk_in, density_in,
    out_adj_now, out_adj_next, out_fwd_now, out_fwd_next, out_bulk, out_density,
    first, second, side, total, flux, lap, beyond, both, bands, bands_in,
    lon_send, lon_recv, lat_send, lat_recv,
    load_sem, lon_ssem, lon_rsem, lat_ssem, lat_rsem, rad_ssem, rad_rsem,
):
    lons, lats, _ = counts
    lon = lax.axis_index("lon")
    lat = lax.axis_index("lat")
    core = lax.axis_index("rad")
    east = lax.rem(lon + 1, lons)
    west = lax.rem(lon + lons - 1, lons)
    other = 1 - core
    has_south = lat > 0
    has_north = lat < lats - 1

    barrier = pltpu.get_barrier_semaphore()

    def greet(where):
        pl.semaphore_signal(barrier, inc=1, device_id=where, device_id_type=MESH)

    greet({"lon": east})
    greet({"lon": west})
    greet({"rad": other})

    @pl.when(has_south)
    def _():
        greet({"lat": lat - 1})

    @pl.when(has_north)
    def _():
        greet({"lat": lat + 1})

    inside = (pl.ds(WIDE, nrad), pl.ds(LOW, nlat))
    sources = (adj_now, fwd_now, buoyancy, stiffness, adj_next, fwd_next, bulk_in, density_in)
    loads = []
    for k, source in enumerate(sources):
        target = first.at[(k,) + inside] if k < 3 else side.at[k - 3]
        loads.append(pltpu.make_async_copy(source, target, load_sem.at[k]))
        loads[-1].start()

    edge = 11 * core
    for block, fields in ((first, 3), (second, 2)):
        for f in range(fields):
            block[f, pl.ds(edge, WIDE)] = jnp.zeros((WIDE, nlat + 16, nlon), jnp.float32)

    @pl.when(jnp.logical_not(has_south))
    def _():
        for step in range(2):
            lat_recv[step, 0] = jnp.zeros(lat_recv.shape[2:], jnp.float32)

    @pl.when(jnp.logical_not(has_north))
    def _():
        for step in range(2):
            lat_recv[step, 1] = jnp.zeros(lat_recv.shape[2:], jnp.float32)

    lane = lax.broadcasted_iota(jnp.int32, (nlat, nlon), 1)
    slot = lax.shift_right_logical(lane * 43, 8)
    low_half = lane - 6 * slot < 3

    def pack(block, fields, step):
        for first_field in range(0, fields, 2):
            edges = jnp.zeros((nlat, nlon), jnp.float32)
            for f in range(first_field, min(first_field + 2, fields)):
                for r in range(nrad):
                    n = (f - first_field) * nrad + r
                    turned = pltpu.roll(
                        block[f, WIDE + r, pl.ds(LOW, nlat)], (6 * n - 125) % 128, 1
                    )
                    edges = jnp.where(slot == n, turned, edges)
            lon_send[step, first_field // 2] = edges
        for f in range(fields):
            for r in range(nrad):
                n = f * nrad + r
                lat_send[step, 0, pl.ds(3 * n, 3)] = block[f, WIDE + r, pl.ds(LOW + nlat - 3, 3)]
                lat_send[step, 1, pl.ds(3 * n, 3)] = block[f, WIDE + r, pl.ds(LOW, 3)]

    def lon_copy(step, way, where):
        parts = pl.ds(0, 2 - step)
        return pltpu.make_async_remote_copy(
            lon_send.at[step, parts], lon_recv.at[step, way, parts],
            lon_ssem.at[step, way], lon_rsem.at[step, way],
            device_id={"lon": where}, device_id_type=MESH,
        )

    def lat_copy(step, way, where, fields):
        rows = pl.ds(0, fields * nrad * 3)
        return pltpu.make_async_remote_copy(
            lat_send.at[step, way, rows], lat_recv.at[step, way, rows],
            lat_ssem.at[step, way], lat_rsem.at[step, way],
            device_id={"lat": where}, device_id_type=MESH,
        )

    def rad_copy(step, block):
        return pltpu.make_async_remote_copy(
            block.at[:, pl.ds(8 - 5 * core, WIDE), pl.ds(LOW, nlat)],
            block.at[:, pl.ds(11 * core, WIDE), pl.ds(LOW, nlat)],
            rad_ssem.at[step], rad_rsem.at[step],
            device_id={"rad": other}, device_id_type=MESH,
        )

    def send(step, block, fields):
        lon_copy(step, 0, east).start()
        lon_copy(step, 1, west).start()

        @pl.when(has_north)
        def _():
            lat_copy(step, 0, lat + 1, fields).start()

        @pl.when(has_south)
        def _():
            lat_copy(step, 1, lat - 1, fields).start()

        rad_copy(step, block).start()

    def wait_rad(step, block):
        rad_copy(step, block).wait_recv()

    def wait_lat(step, fields):
        @pl.when(has_south)
        def _():
            lat_copy(step, 0, lat - 1, fields).wait_recv()

        @pl.when(has_north)
        def _():
            lat_copy(step, 1, lat + 1, fields).wait_recv()

    def wait_lon(step):
        lon_copy(step, 0, west).wait_recv()
        lon_copy(step, 1, east).wait_recv()

    def wait_sent(step, block, fields):
        lon_copy(step, 0, east).wait_send()
        lon_copy(step, 1, west).wait_send()

        @pl.when(has_north)
        def _():
            lat_copy(step, 0, lat + 1, fields).wait_send()

        @pl.when(has_south)
        def _():
            lat_copy(step, 1, lat - 1, fields).wait_send()

        rad_copy(step, block).wait_send()

    def along_rad(block):
        for t in range(nlat // 8):
            rows = pl.ds(LOW + 8 * t, 8)
            adj, fwd, buoy = block[0, :, rows], block[1, :, rows], first[2, :, rows]

            def faces(p):
                return near * (p[2:13] - p[1:12]) + far * (p[3:14] - p[0:11])

            both = buoy[1:12] + buoy[2:13]
            grad_fwd = faces(fwd)
            flux_adj, flux_fwd = both * faces(adj), both * grad_fwd
            product = flux_adj * grad_fwd

            def diverge(q):
                return half_near * (q[2:10] - q[1:9]) + half_far * (q[3:11] - q[0:8])

            here = pl.ds(8 * t, 8)
            total[0, :, here] = diverge(flux_adj)
            total[1, :, here] = diverge(flux_fwd)
            total[2, :, here] = product[1:9] + product[2:10]

    def along_lat(step, block, fields):
        for f in range(fields):
            for r in range(nrad):
                n = f * nrad + r
                block[f, WIDE + r, pl.ds(LOW - 3, 3)] = lat_recv[step, 0, pl.ds(3 * n, 3)]
                block[f, WIDE + r, pl.ds(LOW + nlat, 3)] = lat_recv[step, 1, pl.ds(3 * n, 3)]
        rows = nlat + 8
        for r in range(nrad):
            def at(ref, f, k):
                return ref[f, WIDE + r, pl.ds(LOW - 2 + k, rows)]

            def faces(f):
                return near * (at(block, f, 1) - at(block, f, 0)) + far * (
                    at(block, f, 2) - at(block, f, -1)
                )

            both = at(first, 2, 0) + at(first, 2, 1)
            grad_fwd = faces(1)
            flux_adj = both * faces(0)
            flux[r, 0] = flux_adj
            flux[r, 1] = both * grad_fwd
            flux[r, 2] = flux_adj * grad_fwd

            def moved(f, k):
                return flux[r, f, pl.ds(2 + k, nlat)]

            for f in range(2):
                total[f, r] += half_near * (moved(f, 0) - moved(f, -1)) + half_far * (
                    moved(f, 1) - moved(f, -2)
                )
            total[2, r] += moved(2, 0) + moved(2, -1)

    def ahead(x, h, k):
        return pltpu.roll(jnp.where(lane < k, h, x), 128 - k, 1)

    def behind(x, h, k):
        return pltpu.roll(jnp.where(lane >= 128 - k, h, x), k, 1)

    def fetch_halos(step, fields):
        for f in fields:
            edges = jnp.where(low_half, lon_recv[step, 0, f // 2], lon_recv[step, 1, f // 2])
            for r in range(nrad):
                beyond[f, r] = pltpu.roll(edges, (125 - 6 * ((f % 2) * nrad + r)) % 128, 1)

    ring = 2 * nlon

    def banded(columns, start):
        source = lax.broadcasted_iota(jnp.int32, (ring, columns), 0)
        place = lax.broadcasted_iota(jnp.int32, (ring, columns), 1)
        gap = lax.bitwise_and(source - place - start + ring, ring - 1)
        out = jnp.where(gap == 1, 27.0, 0.0) - jnp.where(gap == 0, 27.0, 0.0)
        out = out - jnp.where(gap == 2, 1.0, 0.0) + jnp.where(gap == ring - 1, 1.0, 0.0)
        return out.astype(jnp.bfloat16)

    def set_bands():
        for k in range(3):
            bands[pl.ds(ring * k, ring)] = banded(ring, 0)
            bands_in[pl.ds(ring * k, ring)] = banded(nlon, -1)

    def times(x, h, matrix):
        parts = []
        rest = (x, h)
        for k in range(3):
            cut = tuple(v.astype(jnp.bfloat16) for v in rest)
            parts.extend(cut)
            if k < 2:
                rest = tuple(v - c.astype(jnp.float32) for v, c in zip(rest, cut))
        return jnp.dot(
            jnp.concatenate(parts, axis=1), matrix[...], preferred_element_type=jnp.float32
        )

    cells = nrad * nlat

    def set_both():
        for r in range(nrad):
            buoy, buoy_h = first[2, WIDE + r, pl.ds(LOW, nlat)], beyond[2, r]
            both[r, :, pl.ds(0, nlon)] = buoy + ahead(buoy, buoy_h, 1)
            both[r, :, pl.ds(nlon, nlon)] = buoy_h + ahead(buoy_h, buoy, 1)

    def along_lon(block):
        weight = both[...].reshape(cells, ring)
        slopes, fluxes = [], []
        for f in range(2):
            x = block[f, pl.ds(WIDE, nrad), pl.ds(LOW, nlat)].reshape(cells, nlon)
            slope = times(x, beyond[f].reshape(cells, nlon), bands)
            q = weight * slope
            lap[f] = times(q[:, :nlon], q[:, nlon:], bands_in).reshape(nrad, nlat, nlon)
            slopes.append(slope)
            fluxes.append(q)
        product = (fluxes[0] * slopes[1]).reshape(nrad, nlat, ring)
        for r in range(nrad):
            here, past = product[r, :, :nlon], product[r, :, nlon:]
            lap[2, r] = here + behind(here, past, 1)

    def close(block, r):
        here = (WIDE + r, pl.ds(LOW, nlat))
        lap_adj = stiff_ref[r] * (total[0, r] + (1 / 1152) * lap[0, r])
        lap_fwd = stiff_ref[r] * (total[1, r] + (1 / 1152) * lap[1, r])
        rho = 0.25 * total[2, r] + (1 / 2304) * lap[2, r]
        return block[(0,) + here], block[(1,) + here], lap_adj, lap_fwd, rho

    stiff_ref, adj_next_ref, fwd_next_ref, bulk_ref, density_ref = (side.at[k] for k in range(5))

    set_bands()
    for k in range(3):
        loads[k].wait()
    pack(first, 3, 0)
    pl.semaphore_wait(barrier, 3 + has_south.astype(jnp.int32) + has_north.astype(jnp.int32))
    send(0, first, 3)
    for k in range(3, 8):
        loads[k].wait()

    wait_rad(0, first)
    along_rad(first)
    wait_lat(0, 3)
    along_lat(0, first, 3)
    wait_lon(0)
    fetch_halos(0, range(3))
    set_both()
    along_lon(first)
    for r in range(nrad):
        adj, fwd, lap_adj, lap_fwd, rho = close(first, r)
        bulk_ref[r] += adj * lap_fwd
        density_ref[r] += rho
        second[0, WIDE + r, pl.ds(LOW, nlat)] = 2.0 * adj - adj_next_ref[r] + lap_adj
        second[1, WIDE + r, pl.ds(LOW, nlat)] = 2.0 * fwd - fwd_next_ref[r] + lap_fwd

    pack(second, 2, 1)
    send(1, second, 2)
    out_adj_next[...] = second[(0,) + inside]
    out_fwd_next[...] = second[(1,) + inside]

    wait_rad(1, second)
    along_rad(second)
    wait_lat(1, 2)
    along_lat(1, second, 2)
    wait_lon(1)
    fetch_halos(1, range(2))
    along_lon(second)
    for r in range(nrad):
        adj, fwd, lap_adj, lap_fwd, rho = close(second, r)
        out_bulk[r] = bulk_ref[r] + adj * lap_fwd
        out_density[r] = density_ref[r] + rho
        out_adj_now[r] = 2.0 * adj - first[0, WIDE + r, pl.ds(LOW, nlat)] + lap_adj
        out_fwd_now[r] = 2.0 * fwd - first[1, WIDE + r, pl.ds(LOW, nlat)] + lap_fwd
    wait_sent(0, first, 3)
    wait_sent(1, second, 2)


def write_out(*refs):
    results, outs, sems = refs[:6], refs[6:12], refs[12]
    copies = [
        pltpu.make_async_copy(result, out, sems.at[k])
        for k, (result, out) in enumerate(zip(results, outs))
    ]
    for copy in copies:
        copy.start()
    for copy in copies:
        copy.wait()


def solution(mesh):
    counts = (mesh.shape["lon"], mesh.shape["lat"], mesh.shape["rad"])

    def shards(*blocks):
        nrad, nlat, nlon = blocks[0].shape
        rows, f32, dma = nlat + 16, jnp.float32, pltpu.SemaphoreType.DMA
        held = pl.pallas_call(
            lambda *refs: kernel(nrad, nlat, nlon, counts, *refs),
            out_shape=(pltpu.VMEM(blocks[0].shape, f32),) * 6,
            in_specs=[pl.BlockSpec(memory_space=pl.ANY)] * 8,
            out_specs=(pl.BlockSpec(memory_space=pltpu.VMEM),) * 6,
            scratch_shapes=[
                pltpu.VMEM((3, nrad + 2 * WIDE, rows, nlon), f32),
                pltpu.VMEM((2, nrad + 2 * WIDE, rows, nlon), f32),
                pltpu.VMEM((5, nrad, nlat, nlon), f32),
                pltpu.VMEM((3, nrad, nlat, nlon), f32),
                pltpu.VMEM((nrad, 3, nlat + 8, nlon), f32),
                pltpu.VMEM((3, nrad, nlat, nlon), f32),
                pltpu.VMEM((3, nrad, nlat, nlon), f32),
                pltpu.VMEM((nrad, nlat, 2 * nlon), f32),
                pltpu.VMEM((6 * nlon, 2 * nlon), jnp.bfloat16),
                pltpu.VMEM((6 * nlon, nlon), jnp.bfloat16),
                pltpu.VMEM((2, 2, nlat, nlon), f32),
                pltpu.VMEM((2, 2, 2, nlat, nlon), f32),
                pltpu.VMEM((2, 2, 9 * nrad, nlon), f32),
                pltpu.VMEM((2, 2, 9 * nrad, nlon), f32),
                dma((8,)),
                dma((2, 2)), dma((2, 2)), dma((2, 2)), dma((2, 2)), dma((2,)), dma((2,)),
            ],
            compiler_params=pltpu.CompilerParams(collective_id=0, has_side_effects=True),
            name="steps",
        )(*blocks)
        return pl.pallas_call(
            write_out,
            out_shape=(jax.ShapeDtypeStruct(blocks[0].shape, f32),) * 6,
            in_specs=[pl.BlockSpec(memory_space=pltpu.VMEM)] * 6,
            out_specs=(pl.BlockSpec(memory_space=pl.ANY),) * 6,
            scratch_shapes=[dma((6,))],
            name="write_out",
        )(*(pltpu.with_memory_space_constraint(x, pltpu.VMEM) for x in held))

    spec = P("rad", "lat", "lon")
    return jax.shard_map(
        shards, mesh=mesh, in_specs=(spec,) * 8, out_specs=(spec,) * 6, check_vma=False
    )
```

```python
import jax
import jax.numpy as jnp
from jax import lax
from jax.experimental import pallas as pl
from jax.experimental.pallas import tpu as pltpu
from jax.sharding import PartitionSpec as P

MESH = pl.DeviceIdType.MESH

near = 9.0 / 8.0
far = -1.0 / 24.0
half_near = near / 2
half_far = far / 2

LAYER = 6
ROW = 8


def kernel(
    nrad, nlat, nlon, counts,
    adj_now, adj_next, fwd_now, fwd_next, stiffness, buoyancy, bulk_in, density_in,
    out_adj_now, out_adj_next, out_fwd_now, out_fwd_next, out_bulk, out_density,
    now, new, bulk, density, total, total_h, flux, lap, both, bands, bands_in,
    lon_send, lon_recv, cross_recv, diag_recv,
    load_sem, lon_ssem, lon_rsem, cross_ssem, cross_rsem, diag_ssem, diag_rsem,
    lat_ssem, lat_rsem, edge_ssem, edge_rsem, rad_ssem, rad_rsem,
):
    lons, lats, _ = counts
    lon = lax.axis_index("lon")
    lat = lax.axis_index("lat")
    core = lax.axis_index("rad")
    sides = (lax.rem(lon + 1, lons), lax.rem(lon + lons - 1, lons))
    other = 1 - core
    has_south = lat > 0
    has_north = lat < lats - 1
    ring = 2 * nlon
    x_half, h_half = pl.ds(0, nlon), pl.ds(nlon, nlon)
    layers, rows = pl.ds(LAYER, nrad), pl.ds(ROW, nlat)

    barrier = pltpu.get_barrier_semaphore()

    def greet(where):
        pl.semaphore_signal(barrier, inc=1, device_id=where, device_id_type=MESH)

    greet({"rad": other})
    for side in sides:
        greet({"lon": side})
        greet({"lon": side, "rad": other})
    for exists, to in ((has_south, lat - 1), (has_north, lat + 1)):

        @pl.when(exists)
        def _():
            greet({"lat": to})
            greet({"lat": to, "rad": other})
            for side in sides:
                greet({"lat": to, "lon": side})

    sources = (adj_now, fwd_now, buoyancy, stiffness, adj_next, fwd_next, bulk_in, density_in)
    targets = tuple(now.at[f, layers, rows, x_half] for f in range(6)) + (bulk, density)
    loads = []
    for k in range(8):
        loads.append(pltpu.make_async_copy(sources[k], targets[k], load_sem.at[k]))
        loads[-1].start()

    outside = pl.ds(3 + 11 * core, 3)
    for f in range(3):
        now[f, outside] = jnp.zeros((3,) + now.shape[2:], jnp.float32)
    for f in range(2):
        new[f, outside, rows, x_half] = jnp.zeros((3, nlat, nlon), jnp.float32)
    for d, exists in enumerate((has_south, has_north)):

        @pl.when(jnp.logical_not(exists))
        def _():
            diag_recv[d] = jnp.zeros(diag_recv.shape[1:], jnp.float32)
            beyond = pl.ds((ROW + nlat) * d, 8)
            for f in range(6):
                now[f, layers, beyond, x_half] = jnp.zeros((nrad, 8, nlon), jnp.float32)
                if f < 3:
                    joint = pl.ds(14 - 11 * core, 3)
                    now[f, joint, beyond, x_half] = jnp.zeros((3, 8, nlon), jnp.float32)

    def banded(columns, start):
        source = lax.broadcasted_iota(jnp.int32, (ring, columns), 0)
        place = lax.broadcasted_iota(jnp.int32, (ring, columns), 1)
        gap = lax.bitwise_and(source - place - start + ring, ring - 1)
        out = jnp.where(gap == 1, 27.0, 0.0) - jnp.where(gap == 0, 27.0, 0.0)
        out = out - jnp.where(gap == 2, 1.0, 0.0) + jnp.where(gap == ring - 1, 1.0, 0.0)
        return out.astype(jnp.bfloat16)

    for k in range(3):
        bands[pl.ds(ring * k, ring)] = banded(ring, 0)
        bands_in[pl.ds(ring * k, ring)] = banded(ring, -1)

    def layer_of(j):
        return LAYER + 7 - j + core * (2 * j - 7)

    def joint_layer(j):
        return 14 + j - core * (9 + 2 * j)

    parts = ([], [])
    for f in range(3):
        for j in range(3):
            parts[0].append((f, j, 6 * len(parts[0]), 6))
    for f in range(2):
        for j in range(3, nrad):
            parts[0].append((f, j, 6 * len(parts[0]), 6))
    for j in range(3, nrad):
        parts[1].append((2, j, 6 * len(parts[1]), 6))
    for f in range(3, 6):
        for j in range(nrad):
            parts[1].append((f, j, 36 + 3 * (len(parts[1]) - 5), 3))
    lane = lax.broadcasted_iota(jnp.int32, (nlat, nlon), 1)
    lane8 = lax.broadcasted_iota(jnp.int32, (8, nlon), 1)

    def pack():
        for part in range(2):
            to_east = jnp.zeros((nlat, nlon), jnp.float32)
            to_west = jnp.zeros((nlat, nlon), jnp.float32)
            for f, j, s, w in parts[part]:
                turned = pltpu.roll(now[f, layer_of(j), rows, x_half], (s + w - 128) % 128, 1)
                to_east = jnp.where((lane >= s) & (lane < s + w), turned, to_east)
                to_west = jnp.where((lane >= s + w) & (lane < s + 2 * w), turned, to_west)
            lon_send[0, part] = to_east
            lon_send[1, part] = to_west

    def unpack():
        for part in range(2):
            for f, j, s, w in parts[part]:
                at = layer_of(j)
                back = (128 - s - w) % 128
                edges = jnp.where(lane < s + w, lon_recv[0, part], lon_recv[1, part])
                now[f, at, rows, h_half] = pltpu.roll(edges, back, 1)
                if f < 3:
                    for d in range(2):
                        corner = jnp.where(
                            lane8 < s + w, diag_recv[d, 0, part], diag_recv[d, 1, part]
                        )
                        now[f, at, pl.ds((ROW + nlat) * d, 8), h_half] = pltpu.roll(corner, back, 1)
                    if j < 3:
                        edges = jnp.where(lane < s + w, cross_recv[0], cross_recv[1])
                        now[f, joint_layer(j), rows, h_half] = pltpu.roll(edges, back, 1)

    def remote(src, dst, ssem, rsem, where):
        return pltpu.make_async_remote_copy(
            src, dst, ssem, rsem, device_id=where, device_id_type=MESH
        )

    def lon_copy(way, side):
        return remote(
            lon_send.at[way], lon_recv.at[way], lon_ssem.at[way], lon_rsem.at[way], {"lon": side}
        )

    def cross_copy(way, side):
        return remote(
            lon_send.at[way, 0], cross_recv.at[way], cross_ssem.at[way], cross_rsem.at[way],
            {"lon": side, "rad": other},
        )

    def diag_copy(d, way, to, side):
        return remote(
            lon_send.at[way, :, pl.ds((nlat - 8) * (1 - d), 8)], diag_recv.at[d, way],
            diag_ssem.at[d, way], diag_rsem.at[d, way], {"lat": to, "lon": side},
        )

    def lat_copy(d, to):
        return remote(
            now.at[:, layers, pl.ds(ROW + (nlat - 8) * (1 - d), 8), x_half],
            now.at[:, layers, pl.ds((ROW + nlat) * d, 8), x_half],
            lat_ssem.at[d], lat_rsem.at[d], {"lat": to},
        )

    def edge_copy(d, to):
        return remote(
            now.at[pl.ds(0, 3), pl.ds(11 - 5 * core, 3), pl.ds(ROW + (nlat - 8) * (1 - d), 8), x_half],
            now.at[pl.ds(0, 3), pl.ds(3 + 11 * core, 3), pl.ds((ROW + nlat) * d, 8), x_half],
            edge_ssem.at[d], edge_rsem.at[d], {"lat": to, "rad": other},
        )

    def rad_copies():
        return (
            remote(
                now.at[pl.ds(0, 3), pl.ds(8 - 2 * core, 6), rows, x_half],
                now.at[pl.ds(0, 3), pl.ds(14 * core, 6), rows, x_half],
                rad_ssem.at[0], rad_rsem.at[0], {"rad": other},
            ),
            remote(
                now.at[pl.ds(3, 3), pl.ds(11 - 5 * core, 3), rows, x_half],
                now.at[pl.ds(3, 3), pl.ds(3 + 11 * core, 3), rows, x_half],
                rad_ssem.at[1], rad_rsem.at[1], {"rad": other},
            ),
        )

    goes = ((has_north, lat + 1), (has_south, lat - 1))
    comes = ((has_south, lat - 1), (has_north, lat + 1))

    def each_lat(pairs, act):
        for d, (exists, to) in enumerate(pairs):

            @pl.when(exists)
            def _():
                act(d, to)

    def send_diag(d, to):
        for way in range(2):
            diag_copy(d, way, to, sides[way]).start()

    def send_lat(d, to):
        edge_copy(d, to).start()
        lat_copy(d, to).start()

    def wait_lat(d, to):
        edge_copy(d, to).wait_recv()
        lat_copy(d, to).wait_recv()

    def wait_diag(d, to):
        for way in range(2):
            diag_copy(d, way, to, sides[1 - way]).wait_recv()

    def wait_sent_lat(d, to):
        edge_copy(d, to).wait_send()
        lat_copy(d, to).wait_send()
        for way in range(2):
            diag_copy(d, way, to, sides[way]).wait_send()

    def along_rad(source, low, n, row, tiles, lanes, into):
        for t in range(tiles):
            here = pl.ds(row + 8 * t, 8)
            adj, fwd = (source[f, pl.ds(low, n + 6), here, lanes] for f in range(2))
            buoy = now[2, pl.ds(low, n + 6), here, lanes]

            def faces(p):
                return near * (p[2 : n + 5] - p[1 : n + 4]) + far * (p[3 : n + 6] - p[0 : n + 3])

            weight = buoy[1 : n + 4] + buoy[2 : n + 5]
            grad_fwd = faces(fwd)
            flux_adj, flux_fwd = weight * faces(adj), weight * grad_fwd
            product = flux_adj * grad_fwd

            def diverge(q):
                return half_near * (q[2 : n + 2] - q[1 : n + 1]) + half_far * (
                    q[3 : n + 3] - q[0:n]
                )

            place = (pl.ds(0, n), pl.ds(8 * t, 8))
            into[(0,) + place] = diverge(flux_adj)
            into[(1,) + place] = diverge(flux_fwd)
            into[(2,) + place] = product[1 : n + 1] + product[2 : n + 2]

    def along_lat(source, low, n, row, count, lanes, into):
        for r in range(n):
            def at(ref, f, k):
                return ref[f, low + r, pl.ds(row - 2 + k, count + 8), lanes]

            def faces(f):
                return near * (at(source, f, 1) - at(source, f, 0)) + far * (
                    at(source, f, 2) - at(source, f, -1)
                )

            weight = at(now, 2, 0) + at(now, 2, 1)
            grad_fwd = faces(1)
            flux_adj = weight * faces(0)
            span = pl.ds(0, count + 8)
            flux[r, 0, span] = flux_adj
            flux[r, 1, span] = weight * grad_fwd
            flux[r, 2, span] = flux_adj * grad_fwd

            def moved(f, k):
                return flux[r, f, pl.ds(2 + k, count)]

            here = pl.ds(0, count)
            for f in range(2):
                into[f, r, here] += half_near * (moved(f, 0) - moved(f, -1)) + half_far * (
                    moved(f, 1) - moved(f, -2)
                )
            into[2, r, here] += moved(2, 0) + moved(2, -1)

    def times(x, matrix):
        cuts = []
        for k in range(3):
            cuts.append(x.astype(jnp.bfloat16))
            if k < 2:
                x = x - cuts[-1].astype(jnp.float32)
        return jnp.dot(
            jnp.concatenate(cuts, axis=1), matrix, preferred_element_type=jnp.float32
        )

    def set_both(low, n, row, count):
        lanes = lax.broadcasted_iota(jnp.int32, (count, nlon), 1)
        for r in range(n):
            here, past = (now[2, low + r, pl.ds(row, count), half] for half in (x_half, h_half))
            mixed = (jnp.where(lanes < 1, past, here), jnp.where(lanes < 1, here, past))
            both[r, :, x_half] = here + pltpu.roll(mixed[0], 127, 1)
            both[r, :, h_half] = past + pltpu.roll(mixed[1], 127, 1)

    def along_lon(source, low, n, row, count, weight, columns):
        cells = n * count
        slopes, fluxes = [], []
        for f in range(2):
            x = source[f, pl.ds(low, n), pl.ds(row, count)].reshape(cells, ring)
            slope = times(x, bands[...])
            q = weight * slope
            done = times(q, bands_in[:, pl.ds(0, columns)])
            lap[f, pl.ds(0, n), pl.ds(0, count), pl.ds(0, columns)] = done.reshape(n, count, columns)
            slopes.append(slope)
            fluxes.append(q)
        lap[2, pl.ds(0, n), pl.ds(0, count)] = (fluxes[0] * slopes[1]).reshape(n, count, ring)

    def density_along_lon(r, first_row):
        here, past = (lap[2, r, pl.ds(first_row, nlat), half] for half in (x_half, h_half))
        return here + pltpu.roll(jnp.where(lane >= 127, past, here), 1, 1)

    for k in range(6):
        loads[k].wait()
    pack()
    lat_count = has_south.astype(jnp.int32) + has_north.astype(jnp.int32)
    pl.semaphore_wait(barrier, 5 + 4 * lat_count)
    for way in range(2):
        lon_copy(way, sides[way]).start()
    for way in range(2):
        cross_copy(way, sides[way]).start()
    each_lat(goes, send_diag)
    for copy in rad_copies():
        copy.start()
    each_lat(goes, send_lat)
    loads[6].wait()
    loads[7].wait()

    base = LAYER - 3 * core
    extra = nrad + 3
    top, tall = ROW - 3, nlat + 8
    for copy in rad_copies():
        copy.wait_recv()
    each_lat(comes, wait_lat)
    along_rad(now, base - 3, extra, top, tall // 8, x_half, total)
    along_lat(now, base, extra, top, tall, x_half, total)
    for way in range(2):
        lon_copy(way, sides[1 - way]).wait_recv()
        cross_copy(way, sides[1 - way]).wait_recv()
    each_lat(comes, wait_diag)
    unpack()
    along_rad(now, LAYER - 3, nrad, ROW, nlat // 8, h_half, total_h)
    along_lat(now, LAYER, nrad, ROW, nlat, h_half, total_h)
    set_both(base, extra, top, tall)
    along_lon(now, base, extra, top, tall, both[...].reshape(extra * tall, ring), ring)

    own = 3 * core

    def advance(f, at, here, half, sums, lap_at):
        slope = now[3, at, here, half] * (sums + (1 / 1152) * lap_at)
        fresh = 2.0 * now[f, at, here, half] - now[4 + f, at, here, half] + slope
        return fresh, slope

    for r in range(extra):
        here = pl.ds(top, tall)
        for f in range(2):
            fresh, _ = advance(f, base + r, here, x_half, total[f, r], lap[f, r, :, x_half])
            new[f, base + r, here, x_half] = fresh
    mine = pl.ds(3, nlat)
    for r in range(nrad):
        for f in range(2):
            fresh, _ = advance(
                f, LAYER + r, rows, h_half, total_h[f, r], lap[f, own + r, mine, h_half]
            )
            new[f, LAYER + r, rows, h_half] = fresh
        slope = now[3, LAYER + r, rows, x_half] * (
            total[1, own + r, mine] + (1 / 1152) * lap[1, own + r, mine, x_half]
        )
        bulk[r] += now[0, LAYER + r, rows, x_half] * slope
        density[r] += 0.25 * total[2, own + r, mine] + (1 / 2304) * density_along_lon(own + r, 3)
        out_adj_next[r] = new[0, LAYER + r, rows, x_half]
        out_fwd_next[r] = new[1, LAYER + r, rows, x_half]

    along_rad(new, LAYER - 3, nrad, ROW, nlat // 8, x_half, total)
    along_lat(new, LAYER, nrad, ROW, nlat, x_half, total)
    weight = both[pl.ds(own, nrad), mine].reshape(nrad * nlat, ring)
    along_lon(new, LAYER, nrad, ROW, nlat, weight, nlon)
    first_rows = pl.ds(0, nlat)
    for r in range(nrad):
        adj, fwd = new[0, LAYER + r, rows, x_half], new[1, LAYER + r, rows, x_half]
        stiff = now[3, LAYER + r, rows, x_half]
        lap_adj = stiff * (total[0, r, first_rows] + (1 / 1152) * lap[0, r, first_rows, x_half])
        lap_fwd = stiff * (total[1, r, first_rows] + (1 / 1152) * lap[1, r, first_rows, x_half])
        out_bulk[r] = bulk[r] + adj * lap_fwd
        out_density[r] = density[r] + (
            0.25 * total[2, r, first_rows] + (1 / 2304) * density_along_lon(r, 0)
        )
        out_adj_now[r] = 2.0 * adj - now[0, LAYER + r, rows, x_half] + lap_adj
        out_fwd_now[r] = 2.0 * fwd - now[1, LAYER + r, rows, x_half] + lap_fwd

    for way in range(2):
        lon_copy(way, sides[way]).wait_send()
        cross_copy(way, sides[way]).wait_send()
    each_lat(goes, wait_sent_lat)
    for copy in rad_copies():
        copy.wait_send()


def write_out(*refs):
    results, outs, sems = refs[:6], refs[6:12], refs[12]
    copies = [
        pltpu.make_async_copy(result, out, sems.at[k])
        for k, (result, out) in enumerate(zip(results, outs))
    ]
    for copy in copies:
        copy.start()
    for copy in copies:
        copy.wait()


def solution(mesh):
    counts = (mesh.shape["lon"], mesh.shape["lat"], mesh.shape["rad"])

    def shards(*blocks):
        nrad, nlat, nlon = blocks[0].shape
        f32, dma, vmem = jnp.float32, pltpu.SemaphoreType.DMA, pltpu.VMEM
        depth, tall, ring = nrad + 12, nlat + 24, 2 * nlon
        held = pl.pallas_call(
            lambda *refs: kernel(nrad, nlat, nlon, counts, *refs),
            out_shape=(vmem(blocks[0].shape, f32),) * 6,
            in_specs=[pl.BlockSpec(memory_space=pl.ANY)] * 8,
            out_specs=(pl.BlockSpec(memory_space=vmem),) * 6,
            scratch_shapes=[
                vmem((6, depth, tall, ring), f32),
                vmem((2, depth, tall, ring), f32),
                vmem((nrad, nlat, nlon), f32),
                vmem((nrad, nlat, nlon), f32),
                vmem((3, nrad + 3, nlat + 8, nlon), f32),
                vmem((3, nrad, nlat, nlon), f32),
                vmem((nrad + 3, 3, nlat + 16, nlon), f32),
                vmem((3, nrad + 3, nlat + 8, ring), f32),
                vmem((nrad + 3, nlat + 8, ring), f32),
                vmem((3 * ring, ring), jnp.bfloat16),
                vmem((3 * ring, ring), jnp.bfloat16),
                vmem((2, 2, nlat, nlon), f32),
                vmem((2, 2, nlat, nlon), f32),
                vmem((2, nlat, nlon), f32),
                vmem((2, 2, 2, 8, nlon), f32),
                dma((8,)), dma((2,)), dma((2,)), dma((2,)), dma((2,)), dma((2, 2)), dma((2, 2)),
                dma((2,)), dma((2,)), dma((2,)), dma((2,)), dma((2,)), dma((2,)),
            ],
            compiler_params=pltpu.CompilerParams(collective_id=0, has_side_effects=True),
            name="steps",
        )(*blocks)
        held = tuple(pltpu.with_memory_space_constraint(x, vmem) for x in held)
        return pl.pallas_call(
            write_out,
            out_shape=(jax.ShapeDtypeStruct(blocks[0].shape, f32),) * 6,
            in_specs=[pl.BlockSpec(memory_space=vmem)] * 6,
            out_specs=(pl.BlockSpec(memory_space=pl.ANY),) * 6,
            scratch_shapes=[dma((6,))],
            name="write_out",
        )(*held)

    spec = P("rad", "lat", "lon")
    return jax.shard_map(
        shards, mesh=mesh, in_specs=(spec,) * 8, out_specs=(spec,) * 6, check_vma=False
    )
```

```python
import jax
import jax.numpy as jnp
from jax import lax
from jax.experimental import pallas as pl
from jax.experimental.pallas import tpu as pltpu
from jax.sharding import PartitionSpec as P

MESH = pl.DeviceIdType.MESH

near = 9.0 / 8.0
far = -1.0 / 24.0
half_near = near / 2
half_far = far / 2

LAYER = 6
ROW = 8


def kernel(
    nrad, nlat, nlon, counts,
    adj_now, adj_next, fwd_now, fwd_next, stiffness, buoyancy, bulk_in, density_in,
    out_adj_now, out_adj_next, out_fwd_now, out_fwd_next, out_bulk, out_density,
    now, new, bulk, density, total, total_h, flux, lap, both, bands, bands_in,
    lon_send, lon_recv, cross_recv, diag_recv, lat_send, lat_recv, edge_recv,
    load_sem, lon_ssem, lon_rsem, cross_ssem, cross_rsem, diag_ssem, diag_rsem,
    lat_ssem, lat_rsem, edge_ssem, edge_rsem, rad_ssem, rad_rsem,
):
    lons, lats, _ = counts
    lon = lax.axis_index("lon")
    lat = lax.axis_index("lat")
    core = lax.axis_index("rad")
    sides = (lax.rem(lon + 1, lons), lax.rem(lon + lons - 1, lons))
    other = 1 - core
    has_south = lat > 0
    has_north = lat < lats - 1
    ring = 2 * nlon
    x_half, h_half = pl.ds(0, nlon), pl.ds(nlon, nlon)
    layers, rows = pl.ds(LAYER, nrad), pl.ds(ROW, nlat)

    barrier = pltpu.get_barrier_semaphore()

    def greet(where):
        pl.semaphore_signal(barrier, inc=1, device_id=where, device_id_type=MESH)

    greet({"rad": other})
    for side in sides:
        greet({"lon": side})
        greet({"lon": side, "rad": other})
    for exists, to in ((has_south, lat - 1), (has_north, lat + 1)):

        @pl.when(exists)
        def _():
            greet({"lat": to})
            greet({"lat": to, "rad": other})
            for side in sides:
                greet({"lat": to, "lon": side})

    sources = (adj_now, fwd_now, buoyancy, stiffness, adj_next, fwd_next, bulk_in, density_in)
    targets = tuple(now.at[f, layers, rows, x_half] for f in range(6)) + (bulk, density)
    loads = []
    for k in range(8):
        loads.append(pltpu.make_async_copy(sources[k], targets[k], load_sem.at[k]))
        loads[-1].start()

    outside = pl.ds(3 + 11 * core, 3)
    for f in range(3):
        now[f, outside] = jnp.zeros((3,) + now.shape[2:], jnp.float32)
    for f in range(2):
        new[f, outside, rows, x_half] = jnp.zeros((3, nlat, nlon), jnp.float32)
    for d, exists in enumerate((has_south, has_north)):

        @pl.when(jnp.logical_not(exists))
        def _():
            diag_recv[d] = jnp.zeros(diag_recv.shape[1:], jnp.float32)
            lat_recv[d] = jnp.zeros(lat_recv.shape[1:], jnp.float32)
            edge_recv[d] = jnp.zeros(edge_recv.shape[1:], jnp.float32)

    def banded(columns, start):
        source = lax.broadcasted_iota(jnp.int32, (ring, columns), 0)
        place = lax.broadcasted_iota(jnp.int32, (ring, columns), 1)
        gap = lax.bitwise_and(source - place - start + ring, ring - 1)
        out = jnp.where(gap == 1, 27.0, 0.0) - jnp.where(gap == 0, 27.0, 0.0)
        out = out - jnp.where(gap == 2, 1.0, 0.0) + jnp.where(gap == ring - 1, 1.0, 0.0)
        return out.astype(jnp.bfloat16)

    for k in range(3):
        bands[pl.ds(ring * k, ring)] = banded(ring, 0)
        bands_in[pl.ds(ring * k, ring)] = banded(ring, -1)

    def layer_of(j):
        return LAYER + 7 - j + core * (2 * j - 7)

    def joint_layer(j):
        return 14 + j - core * (9 + 2 * j)

    parts = ([], [])
    for f in range(3):
        for j in range(3):
            parts[0].append((f, j, 6 * len(parts[0]), 6))
    for f in range(2):
        for j in range(3, nrad):
            parts[0].append((f, j, 6 * len(parts[0]), 6))
    for j in range(3, nrad):
        parts[1].append((2, j, 6 * len(parts[1]), 6))
    for f in range(3, 6):
        for j in range(nrad):
            parts[1].append((f, j, 36 + 3 * (len(parts[1]) - 5), 3))
    lane = lax.broadcasted_iota(jnp.int32, (nlat, nlon), 1)
    lane8 = lax.broadcasted_iota(jnp.int32, (8, nlon), 1)

    def pack():
        for part in range(2):
            to_east = jnp.zeros((nlat, nlon), jnp.float32)
            to_west = jnp.zeros((nlat, nlon), jnp.float32)
            for f, j, s, w in parts[part]:
                turned = pltpu.roll(now[f, layer_of(j), rows, x_half], (s + w - 128) % 128, 1)
                to_east = jnp.where((lane >= s) & (lane < s + w), turned, to_east)
                to_west = jnp.where((lane >= s + w) & (lane < s + 2 * w), turned, to_west)
            lon_send[0, part] = to_east
            lon_send[1, part] = to_west

    lines = []
    for depth, group in ((0, range(3)), (3, range(3)), (0, range(3, 6))):
        for j in range(nrad):
            for f in group:
                lines.append((f, j, depth, pl.ds(3 * len(lines), 3)))

    def pack_rows():
        for f, j, depth, line in lines:
            at = layer_of(j)
            lat_send[0, line] = now[f, at, pl.ds(ROW + nlat - 3 - depth, 3), x_half]
            lat_send[1, line] = now[f, at, pl.ds(ROW + depth, 3), x_half]

    def unpack_rows():
        for k, (f, j, depth, line) in enumerate(lines):
            for d, row in enumerate((ROW - 3 - depth, ROW + nlat + depth)):
                now[f, layer_of(j), pl.ds(row, 3), x_half] = lat_recv[d, line]
                if k < 9:
                    now[f, joint_layer(j), pl.ds(row, 3), x_half] = edge_recv[d, line]

    def unpack():
        for part in range(2):
            for f, j, s, w in parts[part]:
                at = layer_of(j)
                back = (128 - s - w) % 128
                edges = jnp.where(lane < s + w, lon_recv[0, part], lon_recv[1, part])
                now[f, at, rows, h_half] = pltpu.roll(edges, back, 1)
                if f < 3:
                    for d in range(2):
                        corner = jnp.where(
                            lane8 < s + w, diag_recv[d, 0, part], diag_recv[d, 1, part]
                        )
                        now[f, at, pl.ds((ROW + nlat) * d, 8), h_half] = pltpu.roll(corner, back, 1)
                    if j < 3:
                        edges = jnp.where(lane < s + w, cross_recv[0], cross_recv[1])
                        now[f, joint_layer(j), rows, h_half] = pltpu.roll(edges, back, 1)

    def remote(src, dst, ssem, rsem, where):
        return pltpu.make_async_remote_copy(
            src, dst, ssem, rsem, device_id=where, device_id_type=MESH
        )

    def lon_copy(way, side):
        return remote(
            lon_send.at[way], lon_recv.at[way], lon_ssem.at[way], lon_rsem.at[way], {"lon": side}
        )

    def cross_copy(way, side):
        return remote(
            lon_send.at[way, 0], cross_recv.at[way], cross_ssem.at[way], cross_rsem.at[way],
            {"lon": side, "rad": other},
        )

    def diag_copy(d, way, to, side):
        return remote(
            lon_send.at[way, :, pl.ds((nlat - 8) * (1 - d), 8)], diag_recv.at[d, way],
            diag_ssem.at[d, way], diag_rsem.at[d, way], {"lat": to, "lon": side},
        )

    def lat_copy(d, to):
        return remote(
            lat_send.at[d], lat_recv.at[d], lat_ssem.at[d], lat_rsem.at[d], {"lat": to}
        )

    def edge_copy(d, to):
        return remote(
            lat_send.at[d, pl.ds(0, 32)], edge_recv.at[d], edge_ssem.at[d], edge_rsem.at[d],
            {"lat": to, "rad": other},
        )

    def rad_copies():
        return (
            remote(
                now.at[pl.ds(0, 3), pl.ds(8 - 2 * core, 6), rows, x_half],
                now.at[pl.ds(0, 3), pl.ds(14 * core, 6), rows, x_half],
                rad_ssem.at[0], rad_rsem.at[0], {"rad": other},
            ),
            remote(
                now.at[pl.ds(3, 3), pl.ds(11 - 5 * core, 3), rows, x_half],
                now.at[pl.ds(3, 3), pl.ds(3 + 11 * core, 3), rows, x_half],
                rad_ssem.at[1], rad_rsem.at[1], {"rad": other},
            ),
        )

    goes = ((has_north, lat + 1), (has_south, lat - 1))
    comes = ((has_south, lat - 1), (has_north, lat + 1))

    def each_lat(pairs, act):
        for d, (exists, to) in enumerate(pairs):

            @pl.when(exists)
            def _():
                act(d, to)

    def send_diag(d, to):
        for way in range(2):
            diag_copy(d, way, to, sides[way]).start()

    def send_lat(d, to):
        lat_copy(d, to).start()
        edge_copy(d, to).start()

    def wait_lat(d, to):
        edge_copy(d, to).wait_recv()
        lat_copy(d, to).wait_recv()

    def wait_diag(d, to):
        for way in range(2):
            diag_copy(d, way, to, sides[1 - way]).wait_recv()

    def wait_sent_lat(d, to):
        edge_copy(d, to).wait_send()
        lat_copy(d, to).wait_send()
        for way in range(2):
            diag_copy(d, way, to, sides[way]).wait_send()

    def along_rad(source, low, n, starts, lanes, into, skip, drop):
        for start in starts:
            here = pl.ds(start, 8)
            adj, fwd = (source[f, pl.ds(low, n + 6), here, lanes] for f in range(2))
            buoy = now[2, pl.ds(low, n + 6), here, lanes]

            def faces(p):
                return near * (p[2 : n + 5] - p[1 : n + 4]) + far * (p[3 : n + 6] - p[0 : n + 3])

            weight = buoy[1 : n + 4] + buoy[2 : n + 5]
            grad_fwd = faces(fwd)
            flux_adj, flux_fwd = weight * faces(adj), weight * grad_fwd
            product = flux_adj * grad_fwd

            def diverge(q):
                return half_near * (q[2 : n + 2] - q[1 : n + 1]) + half_far * (
                    q[3 : n + 3] - q[0:n]
                )

            place = (pl.ds(skip, n), pl.ds(start - drop, 8))
            into[(0,) + place] = diverge(flux_adj)
            into[(1,) + place] = diverge(flux_fwd)
            into[(2,) + place] = product[1 : n + 1] + product[2 : n + 2]

    def along_lat(source, low, n, row, count, lanes, into, put):
        for r in range(n):
            def at(ref, f, k):
                return ref[f, low + r, pl.ds(row - 2 + k, count + 8), lanes]

            def faces(f):
                return near * (at(source, f, 1) - at(source, f, 0)) + far * (
                    at(source, f, 2) - at(source, f, -1)
                )

            weight = at(now, 2, 0) + at(now, 2, 1)
            grad_fwd = faces(1)
            flux_adj = weight * faces(0)
            span = pl.ds(0, count + 8)
            flux[r, 0, span] = flux_adj
            flux[r, 1, span] = weight * grad_fwd
            flux[r, 2, span] = flux_adj * grad_fwd

            def moved(f, k):
                return flux[r, f, pl.ds(2 + k, count)]

            here = pl.ds(put, count)
            for f in range(2):
                into[f, r, here] += half_near * (moved(f, 0) - moved(f, -1)) + half_far * (
                    moved(f, 1) - moved(f, -2)
                )
            into[2, r, here] += moved(2, 0) + moved(2, -1)

    def times(x, matrix):
        cuts = []
        for k in range(3):
            cuts.append(x.astype(jnp.bfloat16))
            if k < 2:
                x = x - cuts[-1].astype(jnp.float32)
        return jnp.dot(
            jnp.concatenate(cuts, axis=1), matrix, preferred_element_type=jnp.float32
        )

    def set_both(low, n, row, count):
        lanes = lax.broadcasted_iota(jnp.int32, (count, nlon), 1)
        for r in range(n):
            here, past = (now[2, low + r, pl.ds(row, count), half] for half in (x_half, h_half))
            mixed = (jnp.where(lanes < 1, past, here), jnp.where(lanes < 1, here, past))
            both[r, :, x_half] = here + pltpu.roll(mixed[0], 127, 1)
            both[r, :, h_half] = past + pltpu.roll(mixed[1], 127, 1)

    def along_lon(source, low, n, row, count, weight, columns):
        cells = n * count
        slopes, fluxes = [], []
        for f in range(2):
            x = source[f, pl.ds(low, n), pl.ds(row, count)].reshape(cells, ring)
            slope = times(x, bands[...])
            q = weight * slope
            done = times(q, bands_in[:, pl.ds(0, columns)])
            lap[f, pl.ds(0, n), pl.ds(0, count), pl.ds(0, columns)] = done.reshape(n, count, columns)
            slopes.append(slope)
            fluxes.append(q)
        lap[2, pl.ds(0, n), pl.ds(0, count)] = (fluxes[0] * slopes[1]).reshape(n, count, ring)

    def density_along_lon(r, first_row):
        here, past = (lap[2, r, pl.ds(first_row, nlat), half] for half in (x_half, h_half))
        return here + pltpu.roll(jnp.where(lane >= 127, past, here), 1, 1)

    for k in range(6):
        loads[k].wait()
    pack()
    pack_rows()
    lat_count = has_south.astype(jnp.int32) + has_north.astype(jnp.int32)
    pl.semaphore_wait(barrier, 5 + 4 * lat_count)
    for way in range(2):
        lon_copy(way, sides[way]).start()
    for way in range(2):
        cross_copy(way, sides[way]).start()
    each_lat(goes, send_diag)
    each_lat(goes, send_lat)
    for copy in rad_copies():
        copy.start()
    loads[6].wait()
    loads[7].wait()

    base = LAYER - 3 * core
    extra = nrad + 3
    top, tall = ROW - 3, nlat + 8
    own = 3 * core
    for copy in rad_copies():
        copy.wait_recv()
    along_rad(now, base - 3, extra, range(ROW, ROW + nlat, 8), x_half, total, 0, 0)
    each_lat(comes, wait_lat)
    unpack_rows()
    along_rad(now, LAYER - 3, nrad, (0, ROW + nlat), x_half, total, own, 0)
    along_lat(now, base, extra, top, tall, x_half, total, top)
    for way in range(2):
        lon_copy(way, sides[1 - way]).wait_recv()
        cross_copy(way, sides[1 - way]).wait_recv()
    each_lat(comes, wait_diag)
    unpack()
    along_rad(now, LAYER - 3, nrad, range(ROW, ROW + nlat, 8), h_half, total_h, 0, ROW)
    along_lat(now, LAYER, nrad, ROW, nlat, h_half, total_h, 0)
    set_both(base, extra, top, tall)
    along_lon(now, base, extra, top, tall, both[...].reshape(extra * tall, ring), ring)

    def advance(f, at, here, half, sums, lap_at):
        slope = now[3, at, here, half] * (sums + (1 / 1152) * lap_at)
        fresh = 2.0 * now[f, at, here, half] - now[4 + f, at, here, half] + slope
        return fresh, slope

    for r in range(extra):
        here = pl.ds(top, tall)
        for f in range(2):
            fresh, _ = advance(f, base + r, here, x_half, total[f, r, here], lap[f, r, :, x_half])
            new[f, base + r, here, x_half] = fresh
    mine = pl.ds(3, nlat)
    for r in range(nrad):
        for f in range(2):
            fresh, _ = advance(
                f, LAYER + r, rows, h_half, total_h[f, r], lap[f, own + r, mine, h_half]
            )
            new[f, LAYER + r, rows, h_half] = fresh
        slope = now[3, LAYER + r, rows, x_half] * (
            total[1, own + r, rows] + (1 / 1152) * lap[1, own + r, mine, x_half]
        )
        bulk[r] += now[0, LAYER + r, rows, x_half] * slope
        density[r] += 0.25 * total[2, own + r, rows] + (1 / 2304) * density_along_lon(own + r, 3)
        out_adj_next[r] = new[0, LAYER + r, rows, x_half]
        out_fwd_next[r] = new[1, LAYER + r, rows, x_half]

    along_rad(new, LAYER - 3, nrad, range(ROW, ROW + nlat, 8), x_half, total, 0, ROW)
    along_lat(new, LAYER, nrad, ROW, nlat, x_half, total, 0)
    weight = both[pl.ds(own, nrad), mine].reshape(nrad * nlat, ring)
    along_lon(new, LAYER, nrad, ROW, nlat, weight, nlon)
    first_rows = pl.ds(0, nlat)
    for r in range(nrad):
        adj, fwd = new[0, LAYER + r, rows, x_half], new[1, LAYER + r, rows, x_half]
        stiff = now[3, LAYER + r, rows, x_half]
        lap_adj = stiff * (total[0, r, first_rows] + (1 / 1152) * lap[0, r, first_rows, x_half])
        lap_fwd = stiff * (total[1, r, first_rows] + (1 / 1152) * lap[1, r, first_rows, x_half])
        out_bulk[r] = bulk[r] + adj * lap_fwd
        out_density[r] = density[r] + (
            0.25 * total[2, r, first_rows] + (1 / 2304) * density_along_lon(r, 0)
        )
        out_adj_now[r] = 2.0 * adj - now[0, LAYER + r, rows, x_half] + lap_adj
        out_fwd_now[r] = 2.0 * fwd - now[1, LAYER + r, rows, x_half] + lap_fwd

    for way in range(2):
        lon_copy(way, sides[way]).wait_send()
        cross_copy(way, sides[way]).wait_send()
    each_lat(goes, wait_sent_lat)
    for copy in rad_copies():
        copy.wait_send()


def write_out(*refs):
    results, outs, sems = refs[:6], refs[6:12], refs[12]
    copies = [
        pltpu.make_async_copy(result, out, sems.at[k])
        for k, (result, out) in enumerate(zip(results, outs))
    ]
    for copy in copies:
        copy.start()
    for copy in copies:
        copy.wait()


def solution(mesh):
    counts = (mesh.shape["lon"], mesh.shape["lat"], mesh.shape["rad"])

    def shards(*blocks):
        nrad, nlat, nlon = blocks[0].shape
        f32, dma, vmem = jnp.float32, pltpu.SemaphoreType.DMA, pltpu.VMEM
        depth, tall, ring = nrad + 12, nlat + 24, 2 * nlon
        held = pl.pallas_call(
            lambda *refs: kernel(nrad, nlat, nlon, counts, *refs),
            out_shape=(vmem(blocks[0].shape, f32),) * 6,
            in_specs=[pl.BlockSpec(memory_space=pl.ANY)] * 8,
            out_specs=(pl.BlockSpec(memory_space=vmem),) * 6,
            scratch_shapes=[
                vmem((6, depth, tall, ring), f32),
                vmem((2, depth, tall, ring), f32),
                vmem((nrad, nlat, nlon), f32),
                vmem((nrad, nlat, nlon), f32),
                vmem((3, nrad + 3, nlat + 16, nlon), f32),
                vmem((3, nrad, nlat, nlon), f32),
                vmem((nrad + 3, 3, nlat + 16, nlon), f32),
                vmem((3, nrad + 3, nlat + 8, ring), f32),
                vmem((nrad + 3, nlat + 8, ring), f32),
                vmem((3 * ring, ring), jnp.bfloat16),
                vmem((3 * ring, ring), jnp.bfloat16),
                vmem((2, 2, nlat, nlon), f32),
                vmem((2, 2, nlat, nlon), f32),
                vmem((2, nlat, nlon), f32),
                vmem((2, 2, 2, 8, nlon), f32),
                vmem((2, 27 * nrad, nlon), f32),
                vmem((2, 27 * nrad, nlon), f32),
                vmem((2, 32, nlon), f32),
                dma((8,)), dma((2,)), dma((2,)), dma((2,)), dma((2,)), dma((2, 2)), dma((2, 2)),
                dma((2,)), dma((2,)), dma((2,)), dma((2,)), dma((2,)), dma((2,)),
            ],
            compiler_params=pltpu.CompilerParams(collective_id=0, has_side_effects=True),
            name="steps",
        )(*blocks)
        held = tuple(pltpu.with_memory_space_constraint(x, vmem) for x in held)
        return pl.pallas_call(
            write_out,
            out_shape=(jax.ShapeDtypeStruct(blocks[0].shape, f32),) * 6,
            in_specs=[pl.BlockSpec(memory_space=vmem)] * 6,
            out_specs=(pl.BlockSpec(memory_space=pl.ANY),) * 6,
            scratch_shapes=[dma((6,))],
            name="write_out",
        )(*held)

    spec = P("rad", "lat", "lon")
    return jax.shard_map(
        shards, mesh=mesh, in_specs=(spec,) * 8, out_specs=(spec,) * 6, check_vma=False
    )
```

```python
import jax
import jax.numpy as jnp
from jax import lax
from jax.experimental import pallas as pl
from jax.experimental.pallas import tpu as pltpu
from jax.sharding import PartitionSpec as P

MESH = pl.DeviceIdType.MESH

near = 9.0 / 8.0
far = -1.0 / 24.0
half_near = near / 2
half_far = far / 2

LAYER = 6
ROW = 8


def kernel(
    nrad, nlat, nlon, counts,
    adj_now, adj_next, fwd_now, fwd_next, stiffness, buoyancy, bulk_in, density_in,
    out_adj_now, out_adj_next, out_fwd_now, out_fwd_next, out_bulk, out_density,
    now, new, bulk, density, total, total_h, flux, lap, both, bands, bands_in,
    lon_send, lon_recv, cross_recv, diag_recv, lat_send, lat_recv, edge_recv,
    load_sem, lon_ssem, lon_rsem, cross_ssem, cross_rsem, diag_ssem, diag_rsem,
    lat_ssem, lat_rsem, edge_ssem, edge_rsem, rad_ssem, rad_rsem,
):
    lons, lats, _ = counts
    lon = lax.axis_index("lon")
    lat = lax.axis_index("lat")
    core = lax.axis_index("rad")
    sides = (lax.rem(lon + 1, lons), lax.rem(lon + lons - 1, lons))
    other = 1 - core
    has_south = lat > 0
    has_north = lat < lats - 1
    ring = 2 * nlon
    x_half, h_half = pl.ds(0, nlon), pl.ds(nlon, nlon)
    layers, rows = pl.ds(LAYER, nrad), pl.ds(ROW, nlat)

    barrier = pltpu.get_barrier_semaphore()

    def greet(where):
        pl.semaphore_signal(barrier, inc=1, device_id=where, device_id_type=MESH)

    greet({"rad": other})
    for side in sides:
        greet({"lon": side})
        greet({"lon": side, "rad": other})
    for exists, to in ((has_south, lat - 1), (has_north, lat + 1)):

        @pl.when(exists)
        def _():
            greet({"lat": to})
            greet({"lat": to, "rad": other})
            for side in sides:
                greet({"lat": to, "lon": side})

    sources = (adj_now, fwd_now, buoyancy, stiffness, adj_next, fwd_next, bulk_in, density_in)
    targets = tuple(now.at[f, layers, rows, x_half] for f in range(6)) + (bulk, density)
    loads = []
    for k in range(8):
        loads.append(pltpu.make_async_copy(sources[k], targets[k], load_sem.at[k]))
        loads[-1].start()

    outside = pl.ds(3 + 11 * core, 3)
    for f in range(3):
        now[f, outside] = jnp.zeros((3,) + now.shape[2:], jnp.float32)
    for f in range(2):
        new[f, outside, rows, x_half] = jnp.zeros((3, nlat, nlon), jnp.float32)
    for d, exists in enumerate((has_south, has_north)):

        @pl.when(jnp.logical_not(exists))
        def _():
            diag_recv[d] = jnp.zeros(diag_recv.shape[1:], jnp.float32)
            lat_recv[d] = jnp.zeros(lat_recv.shape[1:], jnp.float32)
            edge_recv[d] = jnp.zeros(edge_recv.shape[1:], jnp.float32)

    def banded(columns, start):
        source = lax.broadcasted_iota(jnp.int32, (ring, columns), 0)
        place = lax.broadcasted_iota(jnp.int32, (ring, columns), 1)
        gap = lax.bitwise_and(source - place - start + ring, ring - 1)
        out = jnp.where(gap == 1, 27.0, 0.0) - jnp.where(gap == 0, 27.0, 0.0)
        out = out - jnp.where(gap == 2, 1.0, 0.0) + jnp.where(gap == ring - 1, 1.0, 0.0)
        return out.astype(jnp.bfloat16)

    for k in range(3):
        bands[pl.ds(ring * k, ring)] = banded(ring, 0)
        bands_in[pl.ds(ring * k, ring)] = banded(ring, -1)

    def layer_of(j):
        return LAYER + 7 - j + core * (2 * j - 7)

    def joint_layer(j):
        return 14 + j - core * (9 + 2 * j)

    parts = ([], [])
    for f in range(3):
        for j in range(3):
            parts[0].append((f, j, 6 * len(parts[0]), 6))
    for f in range(2):
        for j in range(3, nrad):
            parts[0].append((f, j, 6 * len(parts[0]), 6))
    for j in range(3, nrad):
        parts[1].append((2, j, 6 * len(parts[1]), 6))
    for f in range(3, 6):
        for j in range(nrad):
            parts[1].append((f, j, 36 + 3 * (len(parts[1]) - 5), 3))
    lane = lax.broadcasted_iota(jnp.int32, (nlat, nlon), 1)
    lane8 = lax.broadcasted_iota(jnp.int32, (8, nlon), 1)

    def pack():
        for part in range(2):
            to_east = jnp.zeros((nlat, nlon), jnp.float32)
            to_west = jnp.zeros((nlat, nlon), jnp.float32)
            for f, j, s, w in parts[part]:
                turned = pltpu.roll(now[f, layer_of(j), rows, x_half], (s + w - 128) % 128, 1)
                to_east = jnp.where((lane >= s) & (lane < s + w), turned, to_east)
                to_west = jnp.where((lane >= s + w) & (lane < s + 2 * w), turned, to_west)
            lon_send[0, part] = to_east
            lon_send[1, part] = to_west

    lines = []
    for depth, group in ((0, range(3)), (3, range(3)), (0, range(3, 6))):
        for j in range(nrad):
            for f in group:
                lines.append((f, j, depth, pl.ds(3 * len(lines), 3)))

    def pack_rows():
        for f, j, depth, line in lines:
            at = layer_of(j)
            lat_send[0, line] = now[f, at, pl.ds(ROW + nlat - 3 - depth, 3), x_half]
            lat_send[1, line] = now[f, at, pl.ds(ROW + depth, 3), x_half]

    def unpack_rows():
        for k, (f, j, depth, line) in enumerate(lines):
            for d, row in enumerate((ROW - 3 - depth, ROW + nlat + depth)):
                now[f, layer_of(j), pl.ds(row, 3), x_half] = lat_recv[d, line]
                if k < 9:
                    now[f, joint_layer(j), pl.ds(row, 3), x_half] = edge_recv[d, line]

    def unpack():
        for part in range(2):
            for f, j, s, w in parts[part]:
                at = layer_of(j)
                back = (128 - s - w) % 128
                edges = jnp.where(lane < s + w, lon_recv[0, part], lon_recv[1, part])
                now[f, at, rows, h_half] = pltpu.roll(edges, back, 1)
                if f < 3:
                    for d in range(2):
                        corner = jnp.where(
                            lane8 < s + w, diag_recv[d, 0, part], diag_recv[d, 1, part]
                        )
                        now[f, at, pl.ds((ROW + nlat) * d, 8), h_half] = pltpu.roll(corner, back, 1)
                    if j < 3:
                        edges = jnp.where(lane < s + w, cross_recv[0], cross_recv[1])
                        now[f, joint_layer(j), rows, h_half] = pltpu.roll(edges, back, 1)

    def remote(src, dst, ssem, rsem, where):
        return pltpu.make_async_remote_copy(
            src, dst, ssem, rsem, device_id=where, device_id_type=MESH
        )

    def lon_copy(way, side):
        return remote(
            lon_send.at[way], lon_recv.at[way], lon_ssem.at[way], lon_rsem.at[way], {"lon": side}
        )

    def cross_copy(way, side):
        return remote(
            lon_send.at[way, 0], cross_recv.at[way], cross_ssem.at[way], cross_rsem.at[way],
            {"lon": side, "rad": other},
        )

    def diag_copy(d, way, to, side):
        return remote(
            lon_send.at[way, :, pl.ds((nlat - 8) * (1 - d), 8)], diag_recv.at[d, way],
            diag_ssem.at[d, way], diag_rsem.at[d, way], {"lat": to, "lon": side},
        )

    def lat_copy(d, to):
        return remote(
            lat_send.at[d], lat_recv.at[d], lat_ssem.at[d], lat_rsem.at[d], {"lat": to}
        )

    def edge_copy(d, to):
        return remote(
            lat_send.at[d, pl.ds(0, 32)], edge_recv.at[d], edge_ssem.at[d], edge_rsem.at[d],
            {"lat": to, "rad": other},
        )

    def rad_copies():
        return (
            remote(
                now.at[pl.ds(0, 3), pl.ds(8 - 2 * core, 6), rows, x_half],
                now.at[pl.ds(0, 3), pl.ds(14 * core, 6), rows, x_half],
                rad_ssem.at[0], rad_rsem.at[0], {"rad": other},
            ),
            remote(
                now.at[pl.ds(3, 3), pl.ds(11 - 5 * core, 3), rows, x_half],
                now.at[pl.ds(3, 3), pl.ds(3 + 11 * core, 3), rows, x_half],
                rad_ssem.at[1], rad_rsem.at[1], {"rad": other},
            ),
        )

    goes = ((has_north, lat + 1), (has_south, lat - 1))
    comes = ((has_south, lat - 1), (has_north, lat + 1))

    def each_lat(pairs, act):
        for d, (exists, to) in enumerate(pairs):

            @pl.when(exists)
            def _():
                act(d, to)

    def send_diag(d, to):
        for way in range(2):
            diag_copy(d, way, to, sides[way]).start()

    def send_lat(d, to):
        lat_copy(d, to).start()
        edge_copy(d, to).start()

    def wait_lat(d, to):
        edge_copy(d, to).wait_recv()
        lat_copy(d, to).wait_recv()

    def wait_diag(d, to):
        for way in range(2):
            diag_copy(d, way, to, sides[1 - way]).wait_recv()

    def wait_sent_lat(d, to):
        edge_copy(d, to).wait_send()
        lat_copy(d, to).wait_send()
        for way in range(2):
            diag_copy(d, way, to, sides[way]).wait_send()

    def along_rad(source, low, n, starts, lanes, into, skip, drop):
        for start in starts:
            here = pl.ds(start, 8)
            adj, fwd = (source[f, pl.ds(low, n + 6), here, lanes] for f in range(2))
            buoy = now[2, pl.ds(low, n + 6), here, lanes]

            def faces(p):
                return near * (p[2 : n + 5] - p[1 : n + 4]) + far * (p[3 : n + 6] - p[0 : n + 3])

            weight = buoy[1 : n + 4] + buoy[2 : n + 5]
            grad_fwd = faces(fwd)
            flux_adj, flux_fwd = weight * faces(adj), weight * grad_fwd
            product = flux_adj * grad_fwd

            def diverge(q):
                return half_near * (q[2 : n + 2] - q[1 : n + 1]) + half_far * (
                    q[3 : n + 3] - q[0:n]
                )

            place = (pl.ds(skip, n), pl.ds(start - drop, 8))
            into[(0,) + place] = diverge(flux_adj)
            into[(1,) + place] = diverge(flux_fwd)
            into[(2,) + place] = product[1 : n + 1] + product[2 : n + 2]

    def along_lat(source, low, n, row, count, lanes, into, put):
        for r in range(n):
            def at(ref, f, k):
                return ref[f, low + r, pl.ds(row - 2 + k, count + 8), lanes]

            def faces(f):
                return near * (at(source, f, 1) - at(source, f, 0)) + far * (
                    at(source, f, 2) - at(source, f, -1)
                )

            weight = at(now, 2, 0) + at(now, 2, 1)
            grad_fwd = faces(1)
            flux_adj = weight * faces(0)
            span = pl.ds(0, count + 8)
            flux[r, 0, span] = flux_adj
            flux[r, 1, span] = weight * grad_fwd
            flux[r, 2, span] = flux_adj * grad_fwd

            def moved(f, k):
                return flux[r, f, pl.ds(2 + k, count)]

            here = pl.ds(put, count)
            for f in range(2):
                into[f, r, here] += half_near * (moved(f, 0) - moved(f, -1)) + half_far * (
                    moved(f, 1) - moved(f, -2)
                )
            into[2, r, here] += moved(2, 0) + moved(2, -1)

    def times(x, matrix):
        cuts = []
        for k in range(3):
            cuts.append(x.astype(jnp.bfloat16))
            if k < 2:
                x = x - cuts[-1].astype(jnp.float32)
        return jnp.dot(
            jnp.concatenate(cuts, axis=1), matrix, preferred_element_type=jnp.float32
        )

    def set_both(low, n, row, count):
        lanes = lax.broadcasted_iota(jnp.int32, (count, nlon), 1)
        for r in range(n):
            here, past = (now[2, low + r, pl.ds(row, count), half] for half in (x_half, h_half))
            mixed = (jnp.where(lanes < 1, past, here), jnp.where(lanes < 1, here, past))
            both[r, :, x_half] = here + pltpu.roll(mixed[0], 127, 1)
            both[r, :, h_half] = past + pltpu.roll(mixed[1], 127, 1)

    def along_lon(source, low, n, row, count, weight, columns):
        cells = n * count
        slopes, fluxes = [], []
        for f in range(2):
            x = source[f, pl.ds(low, n), pl.ds(row, count)].reshape(cells, ring)
            slope = times(x, bands[...])
            q = weight * slope
            done = times(q, bands_in[:, pl.ds(0, columns)])
            lap[f, pl.ds(0, n), pl.ds(0, count), pl.ds(0, columns)] = done.reshape(n, count, columns)
            slopes.append(slope)
            fluxes.append(q)
        lap[2, pl.ds(0, n), pl.ds(0, count)] = (fluxes[0] * slopes[1]).reshape(n, count, ring)

    def density_along_lon(r, first_row):
        here, past = (lap[2, r, pl.ds(first_row, nlat), half] for half in (x_half, h_half))
        return here + pltpu.roll(jnp.where(lane >= 127, past, here), 1, 1)

    for k in range(6):
        loads[k].wait()
    pack()
    pack_rows()
    lat_count = has_south.astype(jnp.int32) + has_north.astype(jnp.int32)
    pl.semaphore_wait(barrier, 5 + 4 * lat_count)
    for way in range(2):
        lon_copy(way, sides[way]).start()
    for way in range(2):
        cross_copy(way, sides[way]).start()
    each_lat(goes, send_diag)
    each_lat(goes, send_lat)
    for copy in rad_copies():
        copy.start()
    loads[6].wait()
    loads[7].wait()

    base = LAYER - 3 * core
    extra = nrad + 3
    top, tall = ROW - 3, nlat + 8
    own = 3 * core
    for copy in rad_copies():
        copy.wait_recv()
    along_rad(now, base - 3, extra, range(ROW, ROW + nlat, 8), x_half, total, 0, 0)
    for way in range(2):
        lon_copy(way, sides[1 - way]).wait_recv()
        cross_copy(way, sides[1 - way]).wait_recv()
    each_lat(comes, wait_diag)
    unpack()
    along_rad(now, LAYER - 3, nrad, range(ROW, ROW + nlat, 8), h_half, total_h, 0, ROW)
    along_lat(now, LAYER, nrad, ROW, nlat, h_half, total_h, 0)
    each_lat(comes, wait_lat)
    unpack_rows()
    along_rad(now, LAYER - 3, nrad, (0, ROW + nlat), x_half, total, own, 0)
    along_lat(now, base, extra, top, tall, x_half, total, top)
    set_both(base, extra, top, tall)
    along_lon(now, base, extra, top, tall, both[...].reshape(extra * tall, ring), ring)

    def advance(f, at, here, half, sums, lap_at):
        slope = now[3, at, here, half] * (sums + (1 / 1152) * lap_at)
        fresh = 2.0 * now[f, at, here, half] - now[4 + f, at, here, half] + slope
        return fresh, slope

    for r in range(extra):
        here = pl.ds(top, tall)
        for f in range(2):
            fresh, _ = advance(f, base + r, here, x_half, total[f, r, here], lap[f, r, :, x_half])
            new[f, base + r, here, x_half] = fresh
    mine = pl.ds(3, nlat)
    for r in range(nrad):
        for f in range(2):
            fresh, _ = advance(
                f, LAYER + r, rows, h_half, total_h[f, r], lap[f, own + r, mine, h_half]
            )
            new[f, LAYER + r, rows, h_half] = fresh
        slope = now[3, LAYER + r, rows, x_half] * (
            total[1, own + r, rows] + (1 / 1152) * lap[1, own + r, mine, x_half]
        )
        bulk[r] += now[0, LAYER + r, rows, x_half] * slope
        density[r] += 0.25 * total[2, own + r, rows] + (1 / 2304) * density_along_lon(own + r, 3)
        out_adj_next[r] = new[0, LAYER + r, rows, x_half]
        out_fwd_next[r] = new[1, LAYER + r, rows, x_half]

    along_rad(new, LAYER - 3, nrad, range(ROW, ROW + nlat, 8), x_half, total, 0, ROW)
    along_lat(new, LAYER, nrad, ROW, nlat, x_half, total, 0)
    weight = both[pl.ds(own, nrad), mine].reshape(nrad * nlat, ring)
    along_lon(new, LAYER, nrad, ROW, nlat, weight, nlon)
    first_rows = pl.ds(0, nlat)
    for r in range(nrad):
        adj, fwd = new[0, LAYER + r, rows, x_half], new[1, LAYER + r, rows, x_half]
        stiff = now[3, LAYER + r, rows, x_half]
        lap_adj = stiff * (total[0, r, first_rows] + (1 / 1152) * lap[0, r, first_rows, x_half])
        lap_fwd = stiff * (total[1, r, first_rows] + (1 / 1152) * lap[1, r, first_rows, x_half])
        out_bulk[r] = bulk[r] + adj * lap_fwd
        out_density[r] = density[r] + (
            0.25 * total[2, r, first_rows] + (1 / 2304) * density_along_lon(r, 0)
        )
        out_adj_now[r] = 2.0 * adj - now[0, LAYER + r, rows, x_half] + lap_adj
        out_fwd_now[r] = 2.0 * fwd - now[1, LAYER + r, rows, x_half] + lap_fwd

    for way in range(2):
        lon_copy(way, sides[way]).wait_send()
        cross_copy(way, sides[way]).wait_send()
    each_lat(goes, wait_sent_lat)
    for copy in rad_copies():
        copy.wait_send()


def write_out(*refs):
    results, outs, sems = refs[:6], refs[6:12], refs[12]
    copies = [
        pltpu.make_async_copy(result, out, sems.at[k])
        for k, (result, out) in enumerate(zip(results, outs))
    ]
    for copy in copies:
        copy.start()
    for copy in copies:
        copy.wait()


def solution(mesh):
    counts = (mesh.shape["lon"], mesh.shape["lat"], mesh.shape["rad"])

    def shards(*blocks):
        nrad, nlat, nlon = blocks[0].shape
        f32, dma, vmem = jnp.float32, pltpu.SemaphoreType.DMA, pltpu.VMEM
        depth, tall, ring = nrad + 12, nlat + 24, 2 * nlon
        held = pl.pallas_call(
            lambda *refs: kernel(nrad, nlat, nlon, counts, *refs),
            out_shape=(vmem(blocks[0].shape, f32),) * 6,
            in_specs=[pl.BlockSpec(memory_space=pl.ANY)] * 8,
            out_specs=(pl.BlockSpec(memory_space=vmem),) * 6,
            scratch_shapes=[
                vmem((6, depth, tall, ring), f32),
                vmem((2, depth, tall, ring), f32),
                vmem((nrad, nlat, nlon), f32),
                vmem((nrad, nlat, nlon), f32),
                vmem((3, nrad + 3, nlat + 16, nlon), f32),
                vmem((3, nrad, nlat, nlon), f32),
                vmem((nrad + 3, 3, nlat + 16, nlon), f32),
                vmem((3, nrad + 3, nlat + 8, ring), f32),
                vmem((nrad + 3, nlat + 8, ring), f32),
                vmem((3 * ring, ring), jnp.bfloat16),
                vmem((3 * ring, ring), jnp.bfloat16),
                vmem((2, 2, nlat, nlon), f32),
                vmem((2, 2, nlat, nlon), f32),
                vmem((2, nlat, nlon), f32),
                vmem((2, 2, 2, 8, nlon), f32),
                vmem((2, 27 * nrad, nlon), f32),
                vmem((2, 27 * nrad, nlon), f32),
                vmem((2, 32, nlon), f32),
                dma((8,)), dma((2,)), dma((2,)), dma((2,)), dma((2,)), dma((2, 2)), dma((2, 2)),
                dma((2,)), dma((2,)), dma((2,)), dma((2,)), dma((2,)), dma((2,)),
            ],
            compiler_params=pltpu.CompilerParams(collective_id=0, has_side_effects=True),
            name="steps",
        )(*blocks)
        held = tuple(pltpu.with_memory_space_constraint(x, vmem) for x in held)
        return pl.pallas_call(
            write_out,
            out_shape=(jax.ShapeDtypeStruct(blocks[0].shape, f32),) * 6,
            in_specs=[pl.BlockSpec(memory_space=vmem)] * 6,
            out_specs=(pl.BlockSpec(memory_space=pl.ANY),) * 6,
            scratch_shapes=[dma((6,))],
            name="write_out",
        )(*held)

    spec = P("rad", "lat", "lon")
    return jax.shard_map(
        shards, mesh=mesh, in_specs=(spec,) * 8, out_specs=(spec,) * 6, check_vma=False
    )
```
